32 devices in a mesh: freq: 16 (over z, y, x), tm: 2 (over core).
Axes of the slice: x: 2, y: 2, z: 4, core: 2. Of those that a mesh axis runs over, the one named last changes fastest.
Arguments:
- spectra: float32 [512, 2048], P('freq', 'tm'), may hold values from -500 to 500
- lead_delay: int32 [9, 512], replicated, may hold values from 0 to 255, as said below
- tail_delay: int32 [9, 512], replicated, may hold values from 0 to 255, as said below
- widths: int32 [16], replicated, may hold values from 1 to 128, as said below
Outputs:
- best_snr: float32 [2048], P('tm')
- trial_peak: float32 [512], P('freq')
The draws below stay inside these ranges and needn't reach their ends.
Inputs may be any that keep to these rules, and one draw needn't show every extreme that they name: At section s with R = 2**s, for row c with d = c mod 2 R, B = min(R, 32) and m = floor(d / (2 B)): lead_delay[s, c] and tail_delay[s, c] both lie in B m to B m + B - 1, and lead_delay[s, c] <= d. `tail_delay`: same rows and bounds as lead_delay. The 16 widths are distinct and one of them is 128.
All inputs are finite; a program needn't handle non-finite values.
Results may differ from the reference program's by a relative error of at most 0.000035.
Values sent between devices are 32-bit elements; how exact they have to be, the bound alone decides.
No kernel may reach another device: no remote copies, remote signals or barrier semaphores. Data moves between devices by JAX's collectives and lax.ppermute only.
A program may use at most 64 MiB of HBM per device.

```python
import math
import jax
import jax.numpy as jnp
from jax import lax

CH_DEV = 32
SECTIONS = 9
CHANNELS = 512
TIME_DEV = 1024
TIME = 2048
BOXES = 16
MAXW = 128


def draw_spectra(key, part):
    subkeys = jax.random.split(key, 3)
    channel_scale = jnp.exp(jax.random.uniform(subkeys[0], (CHANNELS, 1), jnp.float32, 0.0, math.log(10.0)))
    sample_scale = jnp.exp(jax.random.uniform(subkeys[1], (1, TIME), jnp.float32, 0.0, math.log(4.0)))
    rising = 1.0 + 2.0 * jnp.arange(TIME, dtype=jnp.float32)[None, :] / max(TIME - 1, 1)
    values_raw = jax.random.truncated_normal(subkeys[2], -4.0, 4.0, (CHANNELS, TIME), jnp.float32)
    return values_raw * channel_scale * sample_scale * rising


def delay_tables(key):
    columns = jnp.arange(CHANNELS, dtype=jnp.int32)
    leads_all = []
    tails_all = []
    for section_idx in range(SECTIONS):
        rows_in = 2 ** section_idx
        span_rows = min(rows_in, CH_DEV)
        within = columns % (2 * rows_in)
        group_ids = within // (2 * span_rows)
        remainder = within % (2 * span_rows)
        lowest = jnp.maximum(remainder - span_rows + 1, 0)
        highest = jnp.minimum(remainder, span_rows - 1)
        lowest = jnp.minimum(lowest, highest)
        picked = jax.random.randint(jax.random.fold_in(key, section_idx), (CHANNELS,), 0, 1 << 20, jnp.int32)
        offsets = lowest + picked % (highest - lowest + 1)
        leads_all.append(span_rows * group_ids + offsets)
        tails_all.append(span_rows * group_ids + jnp.minimum(remainder - offsets, span_rows - 1))
    return (jnp.stack(leads_all).astype(jnp.int32), jnp.stack(tails_all).astype(jnp.int32))


def draw_lead_delay(key, part):
    return delay_tables(jax.random.fold_in(key, 11))[0]


def draw_tail_delay(key, part):
    return delay_tables(jax.random.fold_in(key, 11))[1]


def draw_widths(key, part):
    shuffled = jax.random.permutation(jax.random.fold_in(key, 3), MAXW - 1)[:BOXES - 1] + 1
    chosen = jnp.concatenate([jnp.full((1,), MAXW, jnp.int32), (MAXW - shuffled).astype(jnp.int32)])
    return jax.random.permutation(jax.random.fold_in(key, 5), chosen).astype(jnp.int32)


def setup_inputs(seed: int = 0) -> dict:
    key_of = jax.random.split(jax.random.key(seed), 5)
    spectra = draw_spectra(jax.random.fold_in(key_of[4], 71), 0)
    lead_delay = draw_lead_delay(jax.random.fold_in(key_of[4], 71), 0)
    tail_delay = draw_tail_delay(jax.random.fold_in(key_of[4], 71), 0)
    widths = draw_widths(jax.random.fold_in(key_of[4], 71), 0)
    return {"spectra": spectra, "lead_delay": lead_delay, "tail_delay": tail_delay, "widths": widths}


eps_var = 1e-06

def shifted_sum(lower_rows, padded, lower_index, upper_index, delays, halo_len, length):
    picked_low = jnp.take(lower_rows, lower_index, axis=0)
    picked_up = jnp.take(padded, upper_index, axis=0)

    def slide_row(row_values, amount):
        return lax.dynamic_slice_in_dim(row_values, halo_len - amount, length)
    moved_rows = jax.vmap(slide_row)(picked_up, delays)
    return picked_low + moved_rows

def box_best(centred, spread, widths, rim_values):
    row_count, length = centred.shape
    segment = min(256, TIME_DEV)
    block_count = length // segment
    extended = jnp.concatenate([rim_values, centred], axis=1)
    leading_rims = extended[:, :length].reshape(row_count, block_count, segment)[:, :, :MAXW]
    blocks = jnp.concatenate([leading_rims, centred.reshape(row_count, block_count, segment)], axis=2)
    prefix = jnp.cumsum(blocks, axis=2)
    upper_sum = prefix[:, :, MAXW:]
    scale_rows = spread[:, None, None]

    def advance(which, running):
        box_width = widths[which]
        lower_sum = lax.dynamic_slice_in_dim(prefix, (MAXW - box_width).astype(jnp.int32), segment, axis=2)
        scores = (upper_sum - lower_sum) / (scale_rows * jnp.sqrt(box_width.astype(jnp.float32)))
        return jnp.maximum(running, scores)
    start_best = jnp.full((row_count, block_count, segment), -jnp.inf, jnp.float32)
    running = lax.fori_loop(0, widths.shape[0], advance, start_best)
    return running.reshape(row_count, length)

def fdmt_section(current, leading, trailing, rows_in):
    halo_len = rows_in - 1
    positions = jnp.arange(CHANNELS, dtype=jnp.int32)
    band_ids = positions // (2 * rows_in)
    lower_index = 2 * band_ids * rows_in + leading
    upper_index = (2 * band_ids + 1) * rows_in + trailing
    padded = jnp.concatenate([jnp.zeros((CHANNELS, halo_len), jnp.float32), current], axis=1)
    rows_block = min(256, CHANNELS)

    def one_block(triple):
        return shifted_sum(current, padded, triple[0], triple[1], triple[2], halo_len, TIME)

    def shaped(values):
        return values.reshape(CHANNELS // rows_block, rows_block)
    result = lax.map(one_block, (shaped(lower_index), shaped(upper_index), shaped(leading)))
    return result.reshape(CHANNELS, TIME)

def reference(spectra, lead_delay, tail_delay, widths):
    current = spectra
    for section_idx in range(SECTIONS):
        current = fdmt_section(current, lead_delay[section_idx], tail_delay[section_idx], 2 ** section_idx)
    rows_block = min(256, CHANNELS)
    blocks = current.reshape(CHANNELS // rows_block, rows_block, TIME)

    def scores_of(block):
        mean_row = lax.optimization_barrier(jnp.sum(block, axis=1, keepdims=True)) / TIME
        centred = block - mean_row
        spread = jnp.sqrt(lax.optimization_barrier(jnp.sum(centred * centred, axis=1)) / TIME + eps_var)
        rim_values = jnp.zeros((rows_block, MAXW), jnp.float32)
        running = box_best(centred, spread, widths, rim_values)
        return (lax.optimization_barrier(jnp.max(running, axis=0)), lax.optimization_barrier(jnp.max(running, axis=1)))
    over_rows, peak_rows = lax.map(scores_of, blocks)
    return (lax.optimization_barrier(jnp.max(over_rows, axis=0)), peak_rows.reshape(CHANNELS))
```

```python
import functools

import jax
import jax.numpy as jnp
from jax import lax
from jax.experimental import pallas as pl
from jax.experimental.pallas import tpu as pltpu
from jax.sharding import PartitionSpec as P

MAXW = 128
LANES = 128
ROWS = 32
PAD = 8

eps_var = 1e-06
VMEM = pl.BlockSpec(memory_space=pltpu.VMEM)
SMEM = pl.BlockSpec(memory_space=pltpu.SMEM)


def xor_permute(value, axis, by):
    return lax.ppermute(value, axis, [(i, i ^ by) for i in range(lax.axis_size(axis))])


def shift_right(value, axis):
    count = lax.axis_size(axis)
    return lax.ppermute(value, axis, [(i, i + 1) for i in range(count - 1)])


def shifted_rows(src, starts, shifts, segs, lane):
    picked = []
    for start, shift in zip(starts, shifts):
        start = start - (shift >> 7)
        picked.append((src[pl.ds(start, segs), :], src[pl.ds(start - 1, segs), :]))
    out = []
    for (here, before), shift in zip(picked, shifts):
        part = shift & (LANES - 1)
        mixed = jnp.where(lane < LANES - part, here, before)
        out.append(pltpu.roll(mixed, part, axis=1))
    return out


def section_rows(src, src_segs, dst, dst_segs, table, rows, group=8):
    drop = src_segs - dst_segs
    lane = lax.broadcasted_iota(jnp.int32, (dst_segs, LANES), 1)

    def do_group(first):
        entries = [table(first + i) for i in range(group)]
        lower = [src[pl.ds(PAD + low * src_segs + drop, dst_segs), :] for low, _, _, _ in entries]
        upper = shifted_rows(
            src,
            [PAD + up * src_segs + drop for _, up, _, _ in entries],
            [delay for _, _, delay, _ in entries],
            dst_segs,
            lane,
        )
        for (_, _, _, to), a, b in zip(entries, lower, upper):
            dst[pl.ds(to, dst_segs), :] = a + b

    for first in range(0, rows, group):
        do_group(first)


def local_kernel(lead, tail, x, left, out, buf_a, buf_b, stage, *, sections, segs, out_segs, main_segs):
    channels = x.shape[0]
    halo = segs - main_segs
    column = lax.axis_index("freq") * channels
    pairs = channels // 2
    buf_a[pl.ds(0, PAD), :] = jnp.zeros((PAD, LANES), jnp.float32)
    buf_b[pl.ds(0, PAD), :] = jnp.zeros((PAD, LANES), jnp.float32)
    for seg in range(segs):
        source, at = (left, main_segs - halo + seg) if seg < halo else (x, seg - halo)
        stage[pl.ds(seg * channels, channels), :] = source[:, pl.ds(at * LANES, LANES)]
    for seg in range(segs):
        first = seg * channels
        summed = stage[pl.ds(first, pairs, stride=2), :] + stage[pl.ds(first + 1, pairs, stride=2), :]
        buf_a[pl.ds(PAD + seg, pairs, stride=segs), :] = summed
    src, dst = buf_a, buf_b
    for section in range(1, sections):
        rows_in = 2**section
        last = section == sections - 1

        def table(k, section=section, rows_in=rows_in, last=last):
            e = lead[section, column + k]
            h = tail[section, column + k]
            band = k // (2 * rows_in)
            if section == 1:
                low, up = 2 * band, 2 * band + 1
            else:
                low, up = 2 * band * rows_in + e, (2 * band + 1) * rows_in + h
            to = k * out_segs if last else PAD + k * segs
            return low, up, e, to

        section_rows(src, segs, out if last else dst, out_segs if last else segs, table, channels)
        src, dst = dst, src


def quad_kernel(lead, tail, own, one, two, three, out, buf_a, buf_b, *, section, segs, mid_segs, out_segs):
    freq = lax.axis_index("freq")
    place = freq % 4
    size = ROWS * segs
    for by, ref in enumerate((own, one, two, three)):
        to = pl.multiple_of(PAD + (place ^ by) * size, 8)
        buf_a[pl.ds(to, size), :] = ref[...]
    buf_a[pl.ds(0, PAD), :] = jnp.zeros((PAD, LANES), jnp.float32)
    buf_b[pl.ds(0, PAD), :] = jnp.zeros((PAD, LANES), jnp.float32)
    base = (freq // 4) * (4 * ROWS)
    half = place // 2

    def first(k):
        band, row = k // ROWS, k % ROWS
        column = base + 2 * ROWS * band + ROWS * half + row
        e = lead[section, column]
        h = tail[section, column]
        return 2 * band * ROWS + e, (2 * band + 1) * ROWS + h, e, PAD + k * mid_segs

    section_rows(buf_a, segs, buf_b, mid_segs, first, 2 * ROWS)

    def second(k):
        column = base + ROWS * place + k
        e = lead[section + 1, column]
        h = tail[section + 1, column]
        return e - ROWS * half, ROWS + h - ROWS * half, e, k * out_segs

    section_rows(buf_b, mid_segs, out, out_segs, second, ROWS)


def order_of(freq, level):
    order = freq % 4
    for bit in range(2, level):
        order = 2 * order + ((freq >> bit) & 1)
    return order


def pair_kernel(lead, tail, own, other, out, buf_a, *, level, section, segs, out_segs):
    freq = lax.axis_index("freq")
    side = (freq >> level) & 1
    order = order_of(freq, level)
    size = ROWS * segs
    buf_a[pl.ds(0, PAD), :] = jnp.zeros((PAD, LANES), jnp.float32)
    buf_a[pl.ds(pl.multiple_of(PAD + side * size, 8), size), :] = own[...]
    buf_a[pl.ds(pl.multiple_of(PAD + (1 - side) * size, 8), size), :] = other[...]
    base = (freq >> (level + 1)) * (2 * 2**section) + ROWS * (2 * order + side)

    def table(k):
        e = lead[section, base + k]
        h = tail[section, base + k]
        return e - ROWS * order, ROWS + h - ROWS * order, e, k * out_segs

    section_rows(buf_a, segs, out, out_segs, table, ROWS)


def final_kernel(lead, tail, widths, *refs, level, section, n_time, main_segs, trials, place_rows):
    own, other = refs[:n_time], refs[n_time : 2 * n_time]
    outs = refs[2 * n_time : 3 * n_time]
    buf, data, back, sums, scale = refs[3 * n_time :]
    freq = lax.axis_index("freq")
    tm = lax.axis_index("tm")
    side = (freq >> level) & 1
    order = order_of(freq, level)
    total_segs = n_time * main_segs
    stride = PAD + total_segs
    zeros = jnp.zeros((PAD, LANES), jnp.float32)
    for row in range(2 * ROWS):
        buf[pl.ds(row * stride, PAD), :] = zeros
    for which, group in ((side, own), (1 - side, other)):
        for by in range(n_time):
            start = which * (ROWS * stride) + PAD + (tm ^ by) * main_segs
            for row in range(ROWS):
                to = pl.multiple_of(start + row * stride, 8)
                buf[pl.ds(to, main_segs), :] = group[by][pl.ds(row * main_segs, main_segs), :]
    final = 2 * order + side
    first_trial = ROWS * final + trials * tm
    base = (freq >> (level + 1)) * (2 * 2**section) + first_trial
    lane = lax.broadcasted_iota(jnp.int32, (total_segs, LANES), 1)
    group = min(trials, 4)
    for start in range(0, trials, group):
        shifts, lows, ups = [], [], []
        for i in range(start, start + group):
            e = lead[section, base + i]
            h = tail[section, base + i]
            shifts.append(e)
            lows.append((e - ROWS * order) * stride + PAD)
            ups.append((ROWS + h - ROWS * order) * stride + PAD)
        lower = [buf[pl.ds(at, total_segs), :] for at in lows]
        upper = shifted_rows(buf, ups, shifts, total_segs, lane)
        for i, a, b in zip(range(start, start + group), lower, upper):
            value = a + b
            data[pl.ds(i * total_segs, total_segs), :] = value
            sums[pl.ds(i, 1), :] = jnp.sum(value, axis=0, keepdims=True)
    total_time = total_segs * LANES
    mean = jnp.sum(sums[...], axis=1, keepdims=True) / total_time
    sums[...] = jnp.broadcast_to(mean, sums.shape)
    for j in range(widths.shape[0]):
        scale[pl.ds(j, 1), :] = jnp.full((1, LANES), widths[j], jnp.int32).astype(jnp.float32)
    scale[...] = 1.0 / jnp.sqrt(scale[...])

    for start in range(0, trials, group):
        values = []
        for i in range(start, start + group):
            centred = data[pl.ds(i * total_segs, total_segs), :] - sums[pl.ds(i, 1), :]
            sums[pl.ds(i, 1), :] = jnp.sum(centred * centred, axis=0, keepdims=True)
            values.append(centred)
        step = 1
        while step < LANES:
            values = [v + jnp.where(lane >= step, pltpu.roll(v, step, axis=1), 0.0) for v in values]
            step *= 2
        for i, v in zip(range(start, start + group), values):
            data[pl.ds(i * total_segs, total_segs), :] = v
            back[pl.ds(i * stride, PAD), :] = zeros
            whole = jnp.broadcast_to(v[:, LANES - 1 :], v.shape)
            back[pl.ds(i * stride + PAD, total_segs), :] = v - whole
    squares = jnp.sum(sums[...], axis=1, keepdims=True)
    inverse = 1.0 / jnp.sqrt(squares / total_time + eps_var)
    sums[...] = jnp.broadcast_to(inverse, sums.shape)

    best_all = jnp.full((total_segs, LANES), -jnp.inf, jnp.float32)
    group = min(trials, 2)
    for start in range(0, trials, group):
        prefixes = [data[pl.ds(i * total_segs, total_segs), :] for i in range(start, start + group)]
        befores = [back[pl.ds(i * stride + PAD - 1, total_segs), :] for i in range(start, start + group)]
        best = [jnp.full((total_segs, LANES), -jnp.inf, jnp.float32)] * group
        for j in range(widths.shape[0]):
            width = widths[j]
            inv_root = scale[pl.ds(j, 1), :]
            mask = lane < LANES - width
            part = width & (LANES - 1)
            for n in range(group):
                ended = pltpu.roll(jnp.where(mask, prefixes[n], befores[n]), part, axis=1)
                best[n] = jnp.maximum(best[n], (prefixes[n] - ended) * inv_root)
        for n in range(group):
            i = start + n
            scores = best[n] * sums[pl.ds(i, 1), :]
            best_all = jnp.maximum(best_all, scores)
            sums[pl.ds(i, 1), :] = jnp.max(scores, axis=0, keepdims=True)
    peaks = jnp.max(sums[...], axis=1, keepdims=True)
    offset = first_trial % LANES
    shape = sums.shape
    spot = lax.broadcasted_iota(jnp.int32, shape, 1) == lax.broadcasted_iota(jnp.int32, shape, 0) + offset
    peak_row = jnp.max(jnp.where(spot, peaks, -jnp.inf), axis=0, keepdims=True)
    data[pl.ds(0, total_segs), :] = best_all
    for by in range(n_time):
        at = pl.multiple_of((tm ^ by) * main_segs, 8)
        outs[by][pl.ds(0, main_segs), :] = data[pl.ds(at, main_segs), :]
        outs[by][pl.ds(main_segs, place_rows), :] = jnp.full((place_rows, LANES), -jnp.inf, jnp.float32)
        outs[by][pl.ds(main_segs + first_trial // LANES, 1), :] = peak_row


def call(kernel, inputs, out_shapes, scratch, name):
    n_tables = 3 if name == "final" else 2
    specs = [SMEM] * n_tables + [VMEM] * (len(inputs) - n_tables)
    outs = [jax.ShapeDtypeStruct(shape, jnp.float32) for shape in out_shapes]
    used = sum(4 * s[0] * s[1] for s in scratch) + sum(4 * v.size for v in inputs) + sum(4 * o.size for o in outs)
    return pl.pallas_call(
        kernel,
        out_shape=outs,
        in_specs=specs,
        out_specs=[VMEM] * len(outs),
        scratch_shapes=[pltpu.VMEM(shape, jnp.float32) for shape in scratch],
        compiler_params=pltpu.CompilerParams(vmem_limit_bytes=used + (2 << 20)),
        name=name,
    )(*inputs)


def shards(spectra, lead_delay, tail_delay, widths):
    channels, span = spectra.shape
    n_freq = lax.axis_size("freq")
    n_time = lax.axis_size("tm")
    freq = lax.axis_index("freq")
    sections = lead_delay.shape[0]
    local = channels.bit_length() - 1
    cross = n_freq.bit_length() - 1
    main_segs = span // LANES
    last = sections - 1

    def segs_before(section):
        need = sum(2**s - 1 for s in range(section, last))
        return main_segs + -(-need // LANES)

    tables = (lead_delay, tail_delay)
    left = shift_right(spectra, "tm")
    segs = segs_before(1)
    out_segs = segs_before(local)
    (current,) = call(
        functools.partial(local_kernel, sections=local, segs=segs, out_segs=out_segs, main_segs=main_segs),
        (*tables, spectra, left),
        [(channels * out_segs, LANES)],
        [(PAD + channels * segs, LANES)] * 2 + [(channels * segs, LANES)],
        "local",
    )
    segs, mid_segs, out_segs = (segs_before(local + i) for i in range(3))
    others = [xor_permute(current, "freq", by) for by in (1, 2, 3)]
    (current,) = call(
        functools.partial(quad_kernel, section=local, segs=segs, mid_segs=mid_segs, out_segs=out_segs),
        (*tables, current, *others),
        [(ROWS * out_segs, LANES)],
        [(PAD + 4 * ROWS * segs, LANES), (PAD + 2 * ROWS * mid_segs, LANES)],
        "quad",
    )
    for level in range(2, cross - 1):
        section = local + level
        segs, out_segs = segs_before(section), segs_before(section + 1)
        other = xor_permute(current, "freq", 1 << level)
        (current,) = call(
            functools.partial(pair_kernel, level=level, section=section, segs=segs, out_segs=out_segs),
            (*tables, current, other),
            [(ROWS * out_segs, LANES)],
            [(PAD + 2 * ROWS * segs, LANES)],
            "pair",
        )
    level = cross - 1
    other = xor_permute(current, "freq", 1 << level)
    owns = [current] + [xor_permute(current, "tm", by) for by in range(1, n_time)]
    others = [other] + [xor_permute(other, "tm", by) for by in range(1, n_time)]
    trials = ROWS // n_time
    total_segs = n_time * main_segs
    stride = PAD + total_segs
    peak_rows = channels * n_freq // LANES
    place_rows = -(-peak_rows // 8) * 8
    chunk = (main_segs + place_rows, LANES)
    pieces = call(
        functools.partial(
            final_kernel,
            level=level,
            section=last,
            n_time=n_time,
            main_segs=main_segs,
            trials=trials,
            place_rows=place_rows,
        ),
        (*tables, widths, *owns, *others),
        [chunk] * n_time,
        [
            (2 * ROWS * stride, LANES),
            (trials * total_segs, LANES),
            (trials * stride, LANES),
            (trials, LANES),
            (widths.shape[0], LANES),
        ],
        "final",
    )
    merged = pieces[0]
    for by in range(1, n_time):
        merged = jnp.maximum(merged, xor_permute(pieces[by], "tm", by))
    level = 0
    while level < cross:
        span_bits = min(2, cross - level)
        received = [xor_permute(merged, "freq", by << level) for by in range(1, 1 << span_bits)]
        for value in received:
            merged = jnp.maximum(merged, value)
        level += span_bits
    best_snr = merged[:main_segs].reshape(span)
    peaks = merged[main_segs : main_segs + peak_rows].reshape(peak_rows * LANES)
    trial_peak = lax.dynamic_slice_in_dim(peaks, freq * channels, channels)
    return (best_snr, trial_peak)


def solution(mesh):
    placed = (P("freq", "tm"), P(), P(), P())
    return jax.shard_map(
        shards, mesh=mesh, in_specs=placed, out_specs=(P("tm"), P("freq")), check_vma=False
    )
```

```python
import functools

import jax
import jax.numpy as jnp
from jax import lax
from jax.experimental import pallas as pl
from jax.experimental.pallas import tpu as pltpu
from jax.sharding import PartitionSpec as P

LANES = 128
ROWS = 32
PAD = 8

eps_var = 1e-06
VMEM = pl.BlockSpec(memory_space=pltpu.VMEM)
ANY = pl.BlockSpec(memory_space=pl.ANY)


def xor_permute(value, axis, by):
    return lax.ppermute(value, axis, [(i, i ^ by) for i in range(lax.axis_size(axis))])


def shift_right(value, axis):
    count = lax.axis_size(axis)
    return lax.ppermute(value, axis, [(i, i + 1) for i in range(count - 1)])


def section_rows(src, src_row, dst, dst_row, segs, rows, table, far, group=16):
    lane = lax.broadcasted_iota(jnp.int32, (segs, LANES), 1)
    for first in range(0, rows, group):
        picked = []
        for k in range(first, min(first + group, rows)):
            low, up, delay = table(k)
            start = src_row(up)
            if far:
                start = start - (delay >> 7)
                delay = delay & (LANES - 1)
            lower = src[pl.ds(src_row(low), segs), :]
            picked.append((k, delay, lower, src[pl.ds(start, segs), :], src[pl.ds(start - 1, segs), :]))
        for k, delay, lower, here, before in picked:
            mixed = jnp.where(lane < LANES - delay, here, before)
            dst[pl.ds(dst_row(k), segs), :] = lower + pltpu.roll(mixed, delay, axis=1)


def window(start):
    return pl.multiple_of((start // LANES) * LANES, LANES)


def order_of(freq, stage):
    order = 0
    for n in range(stage):
        order = 4 * order + ((freq >> (2 * n)) & 3)
    return order


def pair_kernel(x, out, tip, stage, *, halo):
    channels, span = x.shape
    segs = span // LANES
    for seg in range(segs):
        stage[pl.ds(seg * channels, channels), :] = x[:, pl.ds(seg * LANES, LANES)]
    for seg in range(segs):
        first = seg * channels
        half = channels // 2
        summed = stage[pl.ds(first, half, stride=2), :] + stage[pl.ds(first + 1, half, stride=2), :]
        out[pl.ds(seg, half, stride=segs), :] = summed
        if seg >= segs - halo:
            if halo == 1:
                tip[...] = summed
            else:
                tip[pl.ds(seg - segs + halo, half, stride=halo), :] = summed


def join_kernel(main, tip, out, *, segs, main_segs):
    halo = segs - main_segs
    for row in range(main.shape[0] // main_segs):
        out[pl.ds(row * segs, halo), :] = tip[pl.ds(row * halo, halo), :]
        out[pl.ds(row * segs + halo, main_segs), :] = main[pl.ds(row * main_segs, main_segs), :]


def quad_kernel(lead_all, tail_all, *refs, stage, section, local, segs_of):
    inputs, out = refs[:4], refs[4]
    buf_a, buf_b, lead, tail, sems = refs[5:]
    freq = lax.axis_index("freq")
    place = (freq >> (2 * stage)) & 3
    order = order_of(freq, stage)
    rows_in = 2**section
    base = (freq >> (2 * stage + 2)) * (4 * rows_in)
    half_order = 2 * order + place // 2
    starts = [base + ROWS * half_order, base + 2 * rows_in + ROWS * half_order]
    last_start = base + ROWS * (4 * order + place)
    wheres = [base] if local else [*starts, last_start]
    copies = []
    for n, where in enumerate(wheres):
        for table, to in ((lead_all, lead), (tail_all, tail)):
            copies.append(
                pltpu.make_async_copy(table.at[:, pl.ds(window(where), LANES)], to.at[n], sems.at[len(copies)])
            )
    for copy in copies:
        copy.start()
    segs = segs_of(1) if local else segs_of(section)
    size = inputs[0].shape[0]
    buf_a[pl.ds(0, PAD), :] = jnp.zeros((PAD, LANES), jnp.float32)
    buf_b[pl.ds(0, PAD), :] = jnp.zeros((PAD, LANES), jnp.float32)
    for by, ref in enumerate(inputs):
        to = pl.multiple_of(PAD + (place ^ by) * size, 8)
        buf_a[pl.ds(to, size), :] = ref[...]
    for copy in copies:
        copy.wait()
    src, dst = buf_a, buf_b
    for now in range(1, local):
        reach = 2**now

        def local_table(k, now=now, reach=reach):
            e, h = lead[0, now, k], tail[0, now, k]
            band = k // (2 * reach)
            if now == 1:
                return 2 * band, 2 * band + 1, e
            return 2 * band * reach + e, (2 * band + 1) * reach + h, e

        def at_row(row):
            return PAD + row * segs

        section_rows(src, at_row, dst, at_row, segs, 4 * ROWS, local_table, False)
        src, dst = dst, src
    in_segs = segs
    mid_segs, out_segs = segs_of(section + 1), segs_of(section + 2)

    def mid_table(k):
        band = k // ROWS
        if local:
            slot, column = 0, 2 * ROWS * band + ROWS * half_order + k % ROWS
        else:
            slot, column = band, starts[band] % LANES + k % ROWS
        e, h = lead[slot, section, column], tail[slot, section, column]
        return 2 * band * ROWS + e - ROWS * order, (2 * band + 1) * ROWS + h - ROWS * order, e

    section_rows(
        src,
        lambda row: PAD + row * in_segs + in_segs - mid_segs,
        dst,
        lambda row: PAD + row * mid_segs,
        mid_segs,
        2 * ROWS,
        mid_table,
        rows_in > LANES,
    )

    def last_table(k):
        slot = 0 if local else 2
        column = last_start % LANES + k
        e, h = lead[slot, section + 1, column], tail[slot, section + 1, column]
        return e - ROWS * half_order, ROWS + h - ROWS * half_order, e

    section_rows(
        dst,
        lambda row: PAD + row * mid_segs + mid_segs - out_segs,
        out,
        lambda row: row * out_segs,
        out_segs,
        ROWS,
        last_table,
        2 * rows_in > LANES,
    )


def final_kernel(lead_all, tail_all, widths_all, *refs, stage, section, n_time, main_segs, trials, place_rows):
    own, moved = refs[:4], refs[4 : 3 + n_time]
    outs = refs[3 + n_time : 3 + 2 * n_time]
    buf, mid, data, edges, over, scale, lead, tail, widths, sems = refs[3 + 2 * n_time :]
    freq = lax.axis_index("freq")
    tm = lax.axis_index("tm")
    place = (freq >> (2 * stage)) & 3
    order = order_of(freq, stage)
    rows_in = 2**section
    first_trial = 4 * ROWS * order + trials * tm
    half_order = first_trial // (2 * ROWS)
    starts = [ROWS * half_order, 2 * rows_in + ROWS * half_order, first_trial]
    copies = [pltpu.make_async_copy(widths_all, widths, sems.at[0])]
    for n, (where, row) in enumerate(zip(starts, (section, section, section + 1))):
        for table, to in ((lead_all, lead), (tail_all, tail)):
            part = table.at[pl.ds(row, 1), pl.ds(window(where), LANES)]
            copies.append(pltpu.make_async_copy(part, to.at[pl.ds(n, 1)], sems.at[len(copies)]))
    for copy in copies:
        copy.start()
    total_segs = n_time * main_segs
    total_time = total_segs * LANES
    stride = PAD + total_segs
    zeros = jnp.zeros((PAD, LANES), jnp.float32)
    for row in range(4 * ROWS):
        buf[pl.ds(row * stride, PAD), :] = zeros
    for row in range(2 * ROWS):
        mid[pl.ds(row * stride, PAD), :] = zeros
    size = ROWS * main_segs
    for by_band in range(4):
        for by_time in range(n_time):
            start = (place ^ by_band) * (ROWS * stride) + PAD + (tm ^ by_time) * main_segs
            ref, at = (own[by_band], 0) if by_time == 0 else (moved[by_time - 1], by_band * size)
            for row in range(ROWS):
                to = pl.multiple_of(start + row * stride, 8)
                buf[pl.ds(to, main_segs), :] = ref[pl.ds(at + row * main_segs, main_segs), :]
    for copy in copies:
        copy.wait()

    def at_row(row):
        return row * stride + PAD

    def mid_table(k):
        band = k // ROWS
        column = starts[0] % LANES + k % ROWS
        e, h = lead[band, column], tail[band, column]
        return 2 * band * ROWS + e - ROWS * order, (2 * band + 1) * ROWS + h - ROWS * order, e

    section_rows(buf, at_row, mid, at_row, total_segs, 2 * ROWS, mid_table, rows_in > LANES)

    def last_table(k):
        column = first_trial % LANES + k
        e, h = lead[2, column], tail[2, column]
        return e - ROWS * half_order, ROWS + h - ROWS * half_order, e

    def data_row(row):
        return row * total_segs

    section_rows(mid, at_row, data, data_row, total_segs, trials, last_table, 2 * rows_in > LANES)

    def samples(seg):
        return data[pl.ds(seg, trials, stride=total_segs), :]

    total = samples(0)
    for seg in range(1, total_segs):
        total = total + samples(seg)
    mean = jnp.sum(total, axis=1, keepdims=True) / total_time

    row_at = lax.broadcasted_iota(jnp.int32, (2 * LANES, LANES), 0)
    column_at = lax.broadcasted_iota(jnp.int32, (2 * LANES, LANES), 1)
    after = jnp.where(column_at > row_at, -1.0, 0.0)
    upto = jnp.where(column_at <= row_at - LANES, 1.0, 0.0)
    ones = jnp.where(row_at < LANES, after, upto).astype(jnp.bfloat16)
    ones = jnp.concatenate([ones] * 3, axis=1)
    squares = jnp.zeros((trials, LANES), jnp.float32)
    for seg in range(-1, main_segs):
        parts = []
        for part in range(n_time):
            at = part * main_segs + seg
            centred = samples(at) - mean if at >= 0 else jnp.zeros((trials, LANES), jnp.float32)
            if seg >= 0:
                squares = squares + centred * centred
            parts.append(centred)
        values = jnp.concatenate(parts, axis=0)
        terms = []
        for _ in range(3):
            term = values.astype(jnp.bfloat16)
            terms.append(term)
            values = values - term.astype(jnp.float32)
        both = lax.dot_general(
            ones,
            jnp.concatenate(terms, axis=1),
            (((1,), (1,)), ((), ())),
            preferred_element_type=jnp.float32,
        )
        if seg + 1 < main_segs:
            edges[pl.ds((seg + 1) * 2 * LANES, LANES), :] = both[:LANES]
        if seg >= 0:
            edges[pl.ds(seg * 2 * LANES + LANES, LANES), :] = both[LANES:]
    squares = jnp.sum(squares, axis=1, keepdims=True)
    inverse = 1.0 / jnp.sqrt(squares / total_time + eps_var)
    inverse = jnp.concatenate([jnp.broadcast_to(inverse, (trials, LANES))] * n_time, axis=0).T[:8]

    count = widths.shape[0]
    for j in range(count):
        scale[pl.ds(j * 8, 8), :] = jnp.full((8, LANES), widths[j], jnp.int32).astype(jnp.float32)
    scale[...] = 1.0 / jnp.sqrt(scale[...])
    tall = 64

    def spread_rows(value):
        return jnp.concatenate([value] * (tall // 8), axis=0)

    def fold(value):
        out = value[:8]
        for n in range(8, value.shape[0], 8):
            out = jnp.maximum(out, value[n : n + 8])
        return out

    peaks = jnp.full((8, LANES), -jnp.inf, jnp.float32)
    for seg in range(main_segs):
        blocks = []
        for first in range(0, LANES, tall):
            at = seg * 2 * LANES + LANES + first
            ends = edges[pl.ds(at, tall), :]
            best = None
            for j in range(count):
                score = (ends - edges[pl.ds(at - widths[j], tall), :]) * spread_rows(scale[pl.ds(j * 8, 8), :])
                best = score if j == 0 else jnp.maximum(best, score)
            best = best * spread_rows(inverse)
            peaks = jnp.maximum(peaks, fold(best))
            blocks.append(best)
        turned = jnp.concatenate(blocks, axis=0).T
        for part in range(n_time):
            over[pl.ds((part * main_segs + seg) * 8, 8), :] = fold(turned[part * trials : (part + 1) * trials])
    best_all = over[pl.ds(0, total_segs, stride=8), :]
    for n in range(1, 8):
        best_all = jnp.maximum(best_all, over[pl.ds(n, total_segs, stride=8), :])
    buf[pl.ds(0, total_segs), :] = best_all
    peak_row = jnp.max(peaks, axis=0, keepdims=True)
    step = trials
    while step < LANES:
        peak_row = jnp.maximum(peak_row, pltpu.roll(peak_row, step, axis=1))
        step *= 2
    offset = first_trial % LANES
    lane = lax.broadcasted_iota(jnp.int32, (1, LANES), 1)
    peak_row = jnp.where((lane >= offset) & (lane < offset + trials), peak_row, -jnp.inf)
    for by in range(n_time):
        at = pl.multiple_of((tm ^ by) * main_segs, 8)
        outs[by][pl.ds(0, main_segs), :] = buf[pl.ds(at, main_segs), :]
        outs[by][pl.ds(main_segs, place_rows), :] = jnp.full((place_rows, LANES), -jnp.inf, jnp.float32)
        outs[by][pl.ds(main_segs + first_trial // LANES, 1), :] = peak_row


def call(kernel, name, inputs, out_shapes, scratch=(), tables=()):
    outs = [jax.ShapeDtypeStruct(shape, jnp.float32) for shape in out_shapes]
    used = sum(4 * v.size for v in inputs) + sum(4 * o.size for o in outs)
    used += sum(4 * s.shape[0] * s.shape[1] for s in scratch if len(s.shape) == 2)
    return pl.pallas_call(
        kernel,
        out_shape=outs,
        in_specs=[ANY] * len(tables) + [VMEM] * len(inputs),
        out_specs=[VMEM] * len(outs),
        scratch_shapes=list(scratch),
        compiler_params=pltpu.CompilerParams(vmem_limit_bytes=used + (2 << 20)),
        name=name,
    )(*tables, *inputs)


def floats(rows):
    return pltpu.VMEM((rows, LANES), jnp.float32)


def shards(spectra, lead_delay, tail_delay, widths):
    channels, span = spectra.shape
    n_freq = lax.axis_size("freq")
    n_time = lax.axis_size("tm")
    freq = lax.axis_index("freq")
    sections = lead_delay.shape[0]
    local = channels.bit_length() - 1
    stages = (n_freq.bit_length() - 1) // 2
    main_segs = span // LANES
    full_time = sections - 2

    def segs_of(section):
        need = sum(2**s - 1 for s in range(section, full_time))
        return main_segs + -(-need // LANES)

    def smem_windows(count):
        return [pltpu.SMEM((count, sections, LANES), jnp.int32)] * 2

    tables = (lead_delay, tail_delay)
    pairs = channels // 2
    segs = segs_of(1)
    halo = segs - main_segs
    main, tip = call(
        functools.partial(pair_kernel, halo=halo),
        "pairs",
        [spectra],
        [(pairs * main_segs, LANES), (pairs * halo, LANES)],
        [floats(channels * main_segs)],
    )
    (current,) = call(
        functools.partial(join_kernel, segs=segs, main_segs=main_segs),
        "join",
        [main, shift_right(tip, "tm")],
        [(pairs * segs, LANES)],
    )
    for stage in range(stages - 1):
        section = local + 2 * stage
        others = [xor_permute(current, "freq", by << (2 * stage)) for by in (1, 2, 3)]
        windows = 1 if stage == 0 else 3
        rows = 4 * ROWS * (segs_of(1) if stage == 0 else segs_of(section))
        (current,) = call(
            functools.partial(
                quad_kernel,
                stage=stage,
                section=section,
                local=local if stage == 0 else 0,
                segs_of=segs_of,
            ),
            "quad",
            [current, *others],
            [(ROWS * segs_of(section + 2), LANES)],
            [floats(PAD + rows), floats(PAD + rows), *smem_windows(windows), pltpu.SemaphoreType.DMA((2 * windows,))],
            tables,
        )
    stage = stages - 1
    bands = [current] + [xor_permute(current, "freq", by << (2 * stage)) for by in (1, 2, 3)]
    stacked = jnp.concatenate(bands, axis=0)
    arrays = bands + [xor_permute(stacked, "tm", by) for by in range(1, n_time)]
    trials = 4 * ROWS // n_time
    total_segs = n_time * main_segs
    stride = PAD + total_segs
    peak_rows = channels * n_freq // LANES
    place_rows = -(-peak_rows // 8) * 8
    pieces = call(
        functools.partial(
            final_kernel,
            stage=stage,
            section=full_time,
            n_time=n_time,
            main_segs=main_segs,
            trials=trials,
            place_rows=place_rows,
        ),
        "final",
        arrays,
        [(main_segs + place_rows, LANES)] * n_time,
        [
            floats(4 * ROWS * stride),
            floats(2 * ROWS * stride),
            floats(trials * total_segs),
            floats(2 * LANES * main_segs),
            floats(8 * total_segs),
            floats(widths.shape[0] * 8),
            *[pltpu.SMEM((3, LANES), jnp.int32)] * 2,
            pltpu.SMEM(widths.shape, jnp.int32),
            pltpu.SemaphoreType.DMA((7,)),
        ],
        (*tables, widths),
    )
    merged = pieces[0]
    for by in range(1, n_time):
        merged = jnp.maximum(merged, xor_permute(pieces[by], "tm", by))
    for stage in range(stages - 1):
        received = [xor_permute(merged, "freq", by << (2 * stage)) for by in (1, 2, 3)]
        for value in received:
            merged = jnp.maximum(merged, value)
    best_snr = merged[:main_segs].reshape(span)
    peaks = merged[main_segs : main_segs + peak_rows].reshape(peak_rows * LANES)
    trial_peak = lax.dynamic_slice_in_dim(peaks, freq * channels, channels)
    return (best_snr, trial_peak)


def solution(mesh):
    placed = (P("freq", "tm"), P(), P(), P())
    return jax.shard_map(
        shards, mesh=mesh, in_specs=placed, out_specs=(P("tm"), P("freq")), check_vma=False
    )
```

```python
import functools

import jax
import jax.numpy as jnp
from jax import lax
from jax.experimental import pallas as pl
from jax.experimental.pallas import tpu as pltpu
from jax.sharding import PartitionSpec as P

LANES = 128
ROWS = 32
PAD = 8

eps_var = 1e-06
VMEM = pl.BlockSpec(memory_space=pltpu.VMEM)
ANY = pl.BlockSpec(memory_space=pl.ANY)


def xor_permute(value, axis, by):
    return lax.ppermute(value, axis, [(i, i ^ by) for i in range(lax.axis_size(axis))])


def rotate_right(value, axis):
    count = lax.axis_size(axis)
    return lax.ppermute(value, axis, [(i, (i + 1) % count) for i in range(count)])


def section_rows(src, dst, dst_row, segs, rows, table, entry, group=16):
    lane = lax.broadcasted_iota(jnp.int32, (segs, LANES), 1)
    for first in range(0, rows, group):
        picked = []
        for k in range(first, min(first + group, rows)):
            at, column = entry(k)
            start, delay = table[at + 1, column], table[at + 2, column]
            lower = src[pl.ds(table[at, column], segs), :]
            picked.append((k, delay, lower, src[pl.ds(start, segs), :], src[pl.ds(start - 1, segs), :]))
        for k, delay, lower, here, before in picked:
            mixed = jnp.where(lane < LANES - delay, here, before)
            dst[pl.ds(dst_row(k), segs), :] = lower + pltpu.roll(mixed, delay, axis=1)


def window(start):
    return pl.multiple_of((start // LANES) * LANES, LANES)


def order_of(freq, stage):
    order = 0
    for n in range(stage):
        order = 4 * order + ((freq >> (2 * n)) & 3)
    return order


def pair_kernel(x, out, stage):
    channels, span = x.shape
    segs = span // LANES
    half = channels // 2
    for seg in range(segs):
        stage[pl.ds(seg * channels, channels), :] = x[:, pl.ds(seg * LANES, LANES)]
    for seg in range(segs):
        first = seg * channels
        summed = stage[pl.ds(first, half, stride=2), :] + stage[pl.ds(first + 1, half, stride=2), :]
        out[pl.ds(seg, half, stride=segs), :] = summed


def tips_kernel(*refs, main_segs, halo):
    *inputs, out = refs
    rows = inputs[0].shape[0] // main_segs
    for n, ref in enumerate(inputs):
        for seg in range(halo):
            to = (n * halo + seg) * rows
            out[pl.ds(to, rows), :] = ref[pl.ds(main_segs - halo + seg, rows, stride=main_segs), :]


def stage_places(stage, section, freq, trials_first=None):
    order = order_of(freq, stage)
    place = (freq >> (2 * stage)) & 3
    rows_in = 2**section
    base = (freq >> (2 * stage + 2)) * (4 * rows_in)
    last = base + ROWS * (4 * order + place) if trials_first is None else trials_first
    half_order = (last - base) // (2 * ROWS)
    starts = [base + ROWS * half_order, base + 2 * rows_in + ROWS * half_order, last]
    return base, order, half_order, starts


def tables_kernel(lead_all, tail_all, order_after, *refs, stages, sections, local, strides, trials):
    del order_after
    outs, (lead, tail, sems) = refs[:stages], refs[stages:]
    freq = lax.axis_index("freq")
    plans = []
    for stage in range(stages):
        section = local + 2 * stage
        first_trial = None
        if stage == stages - 1:
            first_trial = 4 * ROWS * order_of(freq, stage) + trials * lax.axis_index("tm")
        base, order, half_order, starts = stage_places(stage, section, freq, first_trial)
        plans.append((section, order, half_order, [base] if stage == 0 else starts))
    copies = []
    slot = 0
    for *_, wheres in plans:
        for where in wheres:
            for table, to in ((lead_all, lead), (tail_all, tail)):
                part = table.at[:, pl.ds(window(where), LANES)]
                copies.append(pltpu.make_async_copy(part, to.at[slot], sems.at[len(copies)]))
            slot += 1
    for copy in copies:
        copy.start()
    for copy in copies:
        copy.wait()
    lane = lax.broadcasted_iota(jnp.int32, (1, LANES), 1)
    slot = 0
    for stage, (section, order, half_order, wheres) in enumerate(plans):
        out, at = outs[stage], 0
        jobs = []
        if stage == 0:
            for now in range(1, local):
                band = lane // (2 * 2**now)
                rows = (2 * band, 2 * band + 1) if now == 1 else (2 * band * 2**now, (2 * band + 1) * 2**now)
                jobs.append((slot, now, *rows, now > 1, strides[now]))
            band = lane // (2 * ROWS)
            jobs.append((slot, section, 2 * band * ROWS, (2 * band + 1) * ROWS, True, strides[section]))
            jobs.append((slot, section + 1, -ROWS * half_order, ROWS - ROWS * half_order, True, strides[section + 1]))
        else:
            for band in range(2):
                low = 2 * band * ROWS - ROWS * order
                jobs.append((slot + band, section, low, low + ROWS, True, strides[section]))
            low = -ROWS * half_order
            jobs.append((slot + 2, section + 1, low, low + ROWS, True, strides[section + 1]))
        for where, row, low, up, picks, (stride, ahead) in jobs:
            e, h = lead[where, pl.ds(row, 1), :], tail[where, pl.ds(row, 1), :]
            out[pl.ds(at, 1), :] = (low + e if picks else low) * stride + ahead
            out[pl.ds(at + 1, 1), :] = (up + h if picks else up) * stride + ahead - (e >> 7)
            out[pl.ds(at + 2, 1), :] = e & (LANES - 1)
            at += 3
        slot += len(wheres)


def quad_kernel(packed, *refs, stage, section, local, segs_of):
    inputs, tips, out = refs[:4], refs[4:-5], refs[-5]
    buf_a, buf_b, table, sem = refs[-4:]
    copy = pltpu.make_async_copy(packed, table, sem)
    copy.start()
    freq = lax.axis_index("freq")
    place = (freq >> (2 * stage)) & 3
    _, _, half_order, starts = stage_places(stage, section, freq)
    segs = segs_of(1) if local else segs_of(section)
    size = inputs[0].shape[0]
    buf_a[pl.ds(0, PAD), :] = jnp.zeros((PAD, LANES), jnp.float32)
    buf_b[pl.ds(0, PAD), :] = jnp.zeros((PAD, LANES), jnp.float32)
    for by, ref in enumerate(inputs):
        if not local:
            to = pl.multiple_of(PAD + (place ^ by) * size, 8)
            buf_a[pl.ds(to, size), :] = ref[...]
            continue
        rows = ROWS // 2
        main_segs = size // rows
        halo = segs - main_segs
        to = PAD + (place ^ by) * (rows * segs)
        for seg in range(halo):
            tip = tips[0][pl.ds((by * halo + seg) * rows, rows), :]
            tip = jnp.where(lax.axis_index("tm") > 0, tip, 0.0)
            buf_a[pl.ds(to + seg, rows, stride=segs), :] = tip
        for row in range(rows):
            buf_a[pl.ds(to + row * segs + halo, main_segs), :] = ref[pl.ds(row * main_segs, main_segs), :]
    copy.wait()
    src, dst = buf_a, buf_b
    for now in range(1, local):
        section_rows(
            src,
            dst,
            lambda k: PAD + k * segs,
            segs,
            4 * ROWS,
            table,
            lambda k, now=now: (3 * (now - 1), k),
        )
        src, dst = dst, src
    mid_segs, out_segs = segs_of(section + 1), segs_of(section + 2)

    def mid_entry(k):
        band = k // ROWS
        if local:
            return 3 * (local - 1), 2 * ROWS * band + ROWS * half_order + k % ROWS
        return 3 * band, starts[band] % LANES + k % ROWS

    section_rows(src, dst, lambda k: PAD + k * mid_segs, mid_segs, 2 * ROWS, table, mid_entry)
    at = 3 * local if local else 6
    column = starts[2] % LANES
    section_rows(dst, out, lambda k: k * out_segs, out_segs, ROWS, table, lambda k: (at, column + k))


def final_kernel(packed, widths_all, *refs, stage, section, n_time, main_segs, trials, place_rows):
    own, moved = refs[:4], refs[4 : 3 + n_time]
    outs = refs[3 + n_time : 3 + 2 * n_time]
    buf, mid, data, edges, over, scale, table, widths, sems = refs[3 + 2 * n_time :]
    copies = [
        pltpu.make_async_copy(packed, table, sems.at[0]),
        pltpu.make_async_copy(widths_all, widths, sems.at[1]),
    ]
    for copy in copies:
        copy.start()
    freq = lax.axis_index("freq")
    tm = lax.axis_index("tm")
    place = (freq >> (2 * stage)) & 3
    first_trial = 4 * ROWS * order_of(freq, stage) + trials * tm
    _, _, _, starts = stage_places(stage, section, freq, first_trial)
    total_segs = n_time * main_segs
    total_time = total_segs * LANES
    stride = PAD + total_segs
    zeros = jnp.zeros((PAD, LANES), jnp.float32)
    for row in range(4 * ROWS):
        buf[pl.ds(row * stride, PAD), :] = zeros
    for row in range(2 * ROWS):
        mid[pl.ds(row * stride, PAD), :] = zeros
    size = ROWS * main_segs
    for by_band in range(4):
        for by_time in range(n_time):
            start = (place ^ by_band) * (ROWS * stride) + PAD + (tm ^ by_time) * main_segs
            ref, at = (own[by_band], 0) if by_time == 0 else (moved[by_time - 1], by_band * size)
            for row in range(ROWS):
                to = pl.multiple_of(start + row * stride, 8)
                buf[pl.ds(to, main_segs), :] = ref[pl.ds(at + row * main_segs, main_segs), :]
    for copy in copies:
        copy.wait()

    section_rows(
        buf,
        mid,
        lambda k: PAD + k * stride,
        total_segs,
        2 * ROWS,
        table,
        lambda k: (3 * (k // ROWS), starts[k // ROWS] % LANES + k % ROWS),
    )
    column = first_trial % LANES
    section_rows(mid, data, lambda k: k * total_segs, total_segs, trials, table, lambda k: (6, column + k))

    def samples(seg):
        return data[pl.ds(seg, trials, stride=total_segs), :]

    total = samples(0)
    for seg in range(1, total_segs):
        total = total + samples(seg)
    mean = jnp.sum(total, axis=1, keepdims=True) / total_time

    row_at = lax.broadcasted_iota(jnp.int32, (2 * LANES, LANES), 0)
    column_at = lax.broadcasted_iota(jnp.int32, (2 * LANES, LANES), 1)
    after = jnp.where(column_at > row_at, -1.0, 0.0)
    upto = jnp.where(column_at <= row_at - LANES, 1.0, 0.0)
    ones = jnp.where(row_at < LANES, after, upto).astype(jnp.bfloat16)
    ones = jnp.concatenate([ones] * 3, axis=1)
    squares = jnp.zeros((trials, LANES), jnp.float32)
    for seg in range(-1, main_segs):
        parts = []
        for part in range(n_time):
            at = part * main_segs + seg
            centred = samples(at) - mean if at >= 0 else jnp.zeros((trials, LANES), jnp.float32)
            if seg >= 0:
                squares = squares + centred * centred
            parts.append(centred)
        values = jnp.concatenate(parts, axis=0)
        terms = []
        for _ in range(3):
            term = values.astype(jnp.bfloat16)
            terms.append(term)
            values = values - term.astype(jnp.float32)
        both = lax.dot_general(
            ones,
            jnp.concatenate(terms, axis=1),
            (((1,), (1,)), ((), ())),
            preferred_element_type=jnp.float32,
        )
        if seg + 1 < main_segs:
            edges[pl.ds((seg + 1) * 2 * LANES, LANES), :] = both[:LANES]
        if seg >= 0:
            edges[pl.ds(seg * 2 * LANES + LANES, LANES), :] = both[LANES:]
    squares = jnp.sum(squares, axis=1, keepdims=True)
    inverse = 1.0 / jnp.sqrt(squares / total_time + eps_var)
    inverse = jnp.concatenate([jnp.broadcast_to(inverse, (trials, LANES))] * n_time, axis=0).T[:8]

    count = widths.shape[0]
    for j in range(count):
        scale[pl.ds(j * 8, 8), :] = jnp.full((8, LANES), widths[j], jnp.int32).astype(jnp.float32)
    scale[...] = 1.0 / jnp.sqrt(scale[...])
    tall = 64

    def spread_rows(value):
        return jnp.concatenate([value] * (tall // 8), axis=0)

    def fold(value):
        out = value[:8]
        for n in range(8, value.shape[0], 8):
            out = jnp.maximum(out, value[n : n + 8])
        return out

    peaks = jnp.full((8, LANES), -jnp.inf, jnp.float32)
    for seg in range(main_segs):
        blocks = []
        for first in range(0, LANES, tall):
            at = seg * 2 * LANES + LANES + first
            ends = edges[pl.ds(at, tall), :]
            best = None
            for j in range(count):
                score = (ends - edges[pl.ds(at - widths[j], tall), :]) * spread_rows(scale[pl.ds(j * 8, 8), :])
                best = score if j == 0 else jnp.maximum(best, score)
            best = best * spread_rows(inverse)
            peaks = jnp.maximum(peaks, fold(best))
            blocks.append(best)
        turned = jnp.concatenate(blocks, axis=0).T
        for part in range(n_time):
            over[pl.ds((part * main_segs + seg) * 8, 8), :] = fold(turned[part * trials : (part + 1) * trials])
    best_all = over[pl.ds(0, total_segs, stride=8), :]
    for n in range(1, 8):
        best_all = jnp.maximum(best_all, over[pl.ds(n, total_segs, stride=8), :])
    buf[pl.ds(0, total_segs), :] = best_all
    peak_row = jnp.max(peaks, axis=0, keepdims=True)
    step = trials
    while step < LANES:
        peak_row = jnp.maximum(peak_row, pltpu.roll(peak_row, step, axis=1))
        step *= 2
    offset = first_trial % LANES
    lane = lax.broadcasted_iota(jnp.int32, (1, LANES), 1)
    peak_row = jnp.where((lane >= offset) & (lane < offset + trials), peak_row, -jnp.inf)
    for by in range(n_time):
        at = pl.multiple_of((tm ^ by) * main_segs, 8)
        outs[by][pl.ds(0, main_segs), :] = buf[pl.ds(at, main_segs), :]
        outs[by][pl.ds(main_segs, place_rows), :] = jnp.full((place_rows, LANES), -jnp.inf, jnp.float32)
        outs[by][pl.ds(main_segs + first_trial // LANES, 1), :] = peak_row


def finish_kernel(*refs, main_segs, channels):
    inputs, (best_out, peaks_out), (best, row, peaks, sems) = refs[:-6], refs[-6:-4], refs[-4:]
    merged = inputs[0][...]
    for ref in inputs[1:]:
        merged = jnp.maximum(merged, ref[...])
    best[...] = merged[:main_segs]
    row[...] = merged[main_segs:]
    first = pltpu.make_async_copy(best, best_out, sems.at[0])
    first.start()
    start = lax.axis_index("freq") * channels
    mine = pltpu.roll(row[pl.ds(start // LANES, 1), :], (LANES - start % LANES) % LANES, axis=1)
    peaks[...] = mine[:, :channels]
    second = pltpu.make_async_copy(peaks, peaks_out, sems.at[1])
    second.start()
    first.wait()
    second.wait()


def call(kernel, name, inputs, out_shapes, scratch=(), tables=(), out_specs=VMEM, dtype=jnp.float32):
    outs = [jax.ShapeDtypeStruct(shape, dtype) for shape in out_shapes]
    used = sum(4 * v.size for v in inputs) + sum(4 * o.size for o in outs)
    used += sum(4 * s.shape[0] * s.shape[1] for s in scratch if len(s.shape) == 2)
    return pl.pallas_call(
        kernel,
        out_shape=outs,
        in_specs=[ANY] * len(tables) + [VMEM] * len(inputs),
        out_specs=[out_specs] * len(outs),
        scratch_shapes=list(scratch),
        compiler_params=pltpu.CompilerParams(vmem_limit_bytes=used + (2 << 20)),
        name=name,
    )(*tables, *inputs)


def floats(rows):
    return pltpu.VMEM((rows, LANES), jnp.float32)


def shards(spectra, lead_delay, tail_delay, widths):
    channels, span = spectra.shape
    n_freq = lax.axis_size("freq")
    n_time = lax.axis_size("tm")
    freq = lax.axis_index("freq")
    sections = lead_delay.shape[0]
    local = channels.bit_length() - 1
    stages = (n_freq.bit_length() - 1) // 2
    main_segs = span // LANES
    full_time = sections - 2

    def segs_of(section):
        need = sum(2**s - 1 for s in range(section, full_time))
        return main_segs + -(-need // LANES)

    pairs = channels // 2
    segs = segs_of(1)
    halo = segs - main_segs
    (current,) = call(
        pair_kernel,
        "pairs",
        [spectra],
        [(pairs * main_segs, LANES)],
        [floats(channels * main_segs)],
    )
    trials = 4 * ROWS // n_time
    total_segs = n_time * main_segs
    stride = PAD + total_segs
    strides = {}
    for section in range(1, sections):
        if section >= full_time:
            strides[section] = (stride, PAD)
        elif section < local:
            strides[section] = (segs, PAD)
        else:
            strides[section] = (segs_of(section), PAD + segs_of(section) - segs_of(section + 1))
    strides[local] = (segs, PAD + segs - segs_of(local + 1))
    windows = 1 + 3 * (stages - 1)
    tables = call(
        functools.partial(
            tables_kernel, stages=stages, sections=sections, local=local, strides=strides, trials=trials
        ),
        "tables",
        [current],
        [(3 * (local + 1), LANES)] + [(9, LANES)] * (stages - 1),
        [pltpu.VMEM((windows, sections, LANES), jnp.int32)] * 2 + [pltpu.SemaphoreType.DMA((2 * windows,))],
        (lead_delay, tail_delay),
        dtype=jnp.int32,
    )
    for stage in range(stages - 1):
        section = local + 2 * stage
        others = [xor_permute(current, "freq", by << (2 * stage)) for by in (1, 2, 3)]
        inputs = [current, *others]
        if stage == 0:
            (tips,) = call(
                functools.partial(tips_kernel, main_segs=main_segs, halo=halo),
                "tips",
                inputs,
                [(4 * pairs * halo, LANES)],
            )
            inputs.append(rotate_right(tips, "tm"))
        rows = 4 * ROWS * (segs_of(1) if stage == 0 else segs_of(section))
        (current,) = call(
            functools.partial(
                quad_kernel,
                stage=stage,
                section=section,
                local=local if stage == 0 else 0,
                segs_of=segs_of,
            ),
            "quad",
            inputs,
            [(ROWS * segs_of(section + 2), LANES)],
            [
                floats(PAD + rows),
                floats(PAD + rows),
                pltpu.SMEM(tables[stage].shape, jnp.int32),
                pltpu.SemaphoreType.DMA(()),
            ],
            [tables[stage]],
        )
    stage = stages - 1
    two = xor_permute(current, "freq", 2 << (2 * stage))
    one = xor_permute(current, "freq", 1 << (2 * stage))
    three = xor_permute(two, "freq", 1 << (2 * stage))
    bands = [current, one, two, three]
    stacked = jnp.concatenate(bands, axis=0)
    arrays = bands + [xor_permute(stacked, "tm", by) for by in range(1, n_time)]
    peak_rows = channels * n_freq // LANES
    place_rows = -(-peak_rows // 8) * 8
    pieces = call(
        functools.partial(
            final_kernel,
            stage=stage,
            section=full_time,
            n_time=n_time,
            main_segs=main_segs,
            trials=trials,
            place_rows=place_rows,
        ),
        "final",
        arrays,
        [(main_segs + place_rows, LANES)] * n_time,
        [
            floats(4 * ROWS * stride),
            floats(2 * ROWS * stride),
            floats(trials * total_segs),
            floats(2 * LANES * main_segs),
            floats(8 * total_segs),
            floats(widths.shape[0] * 8),
            pltpu.SMEM(tables[stage].shape, jnp.int32),
            pltpu.SMEM(widths.shape, jnp.int32),
            pltpu.SemaphoreType.DMA((2,)),
        ],
        [tables[stage], widths],
    )
    merged = pieces[0]
    for by in range(1, n_time):
        merged = jnp.maximum(merged, xor_permute(pieces[by], "tm", by))
    for stage in range(stages - 1):
        received = [merged] + [xor_permute(merged, "freq", by << (2 * stage)) for by in (1, 2, 3)]
        if stage < stages - 2:
            merged = functools.reduce(jnp.maximum, received)
    best_snr, trial_peak = call(
        functools.partial(finish_kernel, main_segs=main_segs, channels=channels),
        "finish",
        received,
        [(main_segs, LANES), (1, channels)],
        [
            floats(main_segs),
            floats(place_rows),
            pltpu.VMEM((1, channels), jnp.float32),
            pltpu.SemaphoreType.DMA((2,)),
        ],
        out_specs=ANY,
    )
    return (best_snr.reshape(span), trial_peak.reshape(channels))


def solution(mesh):
    placed = (P("freq", "tm"), P(), P(), P())
    return jax.shard_map(
        shards, mesh=mesh, in_specs=placed, out_specs=(P("tm"), P("freq")), check_vma=False
    )
```

```python
import functools

import jax
import jax.numpy as jnp
from jax import lax
from jax.experimental import pallas as pl
from jax.experimental.pallas import tpu as pltpu
from jax.sharding import PartitionSpec as P

LANES = 128
ROWS = 32
PAD = 8

eps_var = 1e-06
VMEM = pl.BlockSpec(memory_space=pltpu.VMEM)
ANY = pl.BlockSpec(memory_space=pl.ANY)


def xor_permute(value, axis, by):
    return lax.ppermute(value, axis, [(i, i ^ by) for i in range(lax.axis_size(axis))])


def section_rows(src, dst, dst_row, segs, rows, table, entry, group=16):
    lane = lax.broadcasted_iota(jnp.int32, (segs, LANES), 1)
    for first in range(0, rows, group):
        picked = []
        for k in range(first, min(first + group, rows)):
            at, column = entry(k)
            start, delay = table[at + 1, column], table[at + 2, column]
            lower = src[pl.ds(table[at, column], segs), :]
            picked.append((k, delay, lower, src[pl.ds(start, segs), :], src[pl.ds(start - 1, segs), :]))
        for k, delay, lower, here, before in picked:
            mixed = jnp.where(lane < LANES - delay, here, before)
            dst[pl.ds(dst_row(k), segs), :] = lower + pltpu.roll(mixed, delay, axis=1)


def window(start):
    return pl.multiple_of((start // LANES) * LANES, LANES)


def order_of(freq, stage):
    order = 0
    for n in range(stage):
        order = 4 * order + ((freq >> (2 * n)) & 3)
    return order


def pair_kernel(x, out, stage):
    channels, span = x.shape
    segs = span // LANES
    half = channels // 2
    for seg in range(segs):
        stage[pl.ds(seg * channels, channels), :] = x[:, pl.ds(seg * LANES, LANES)]
    for seg in range(segs):
        first = seg * channels
        summed = stage[pl.ds(first, half, stride=2), :] + stage[pl.ds(first + 1, half, stride=2), :]
        out[pl.ds(seg, half, stride=segs), :] = summed


def stage_places(stage, section, freq, trials_first=None):
    order = order_of(freq, stage)
    place = (freq >> (2 * stage)) & 3
    rows_in = 2**section
    base = (freq >> (2 * stage + 2)) * (4 * rows_in)
    last = base + ROWS * (4 * order + place) if trials_first is None else trials_first
    half_order = (last - base) // (2 * ROWS)
    starts = [base + ROWS * half_order, base + 2 * rows_in + ROWS * half_order, last]
    return base, order, half_order, starts


def tables_kernel(lead_all, tail_all, order_after, *refs, stages, sections, local, strides, trials):
    del order_after
    outs, (lead, tail, sems) = refs[:stages], refs[stages:]
    freq = lax.axis_index("freq")
    plans = []
    for stage in range(stages):
        section = local + 2 * stage
        first_trial = None
        if stage == stages - 1:
            first_trial = 4 * ROWS * order_of(freq, stage) + trials * lax.axis_index("tm")
        base, order, half_order, starts = stage_places(stage, section, freq, first_trial)
        plans.append((section, order, half_order, [base] if stage == 0 else starts))
    copies = []
    slot = 0
    for *_, wheres in plans:
        for where in wheres:
            for table, to in ((lead_all, lead), (tail_all, tail)):
                part = table.at[:, pl.ds(window(where), LANES)]
                copies.append(pltpu.make_async_copy(part, to.at[slot], sems.at[len(copies)]))
            slot += 1
    for copy in copies:
        copy.start()
    for copy in copies:
        copy.wait()
    lane = lax.broadcasted_iota(jnp.int32, (1, LANES), 1)
    slot = 0
    for stage, (section, order, half_order, wheres) in enumerate(plans):
        out, at = outs[stage], 0
        jobs = []
        if stage == 0:
            for now in range(1, local):
                band = lane // (2 * 2**now)
                rows = (2 * band, 2 * band + 1) if now == 1 else (2 * band * 2**now, (2 * band + 1) * 2**now)
                jobs.append((slot, now, *rows, now > 1, strides[now]))
            band = lane // (2 * ROWS)
            jobs.append((slot, section, 2 * band * ROWS, (2 * band + 1) * ROWS, True, strides[section]))
            jobs.append((slot, section + 1, -ROWS * half_order, ROWS - ROWS * half_order, True, strides[section + 1]))
        else:
            for band in range(2):
                low = 2 * band * ROWS - ROWS * order
                jobs.append((slot + band, section, low, low + ROWS, True, strides[section]))
            low = -ROWS * half_order
            jobs.append((slot + 2, section + 1, low, low + ROWS, True, strides[section + 1]))
        for where, row, low, up, picks, (stride, ahead) in jobs:
            e, h = lead[where, pl.ds(row, 1), :], tail[where, pl.ds(row, 1), :]
            out[pl.ds(at, 1), :] = (low + e if picks else low) * stride + ahead
            out[pl.ds(at + 1, 1), :] = (up + h if picks else up) * stride + ahead - (e >> 7)
            out[pl.ds(at + 2, 1), :] = e & (LANES - 1)
            at += 3
        slot += len(wheres)


def quad_kernel(packed, *refs, stage, section, local, ahead, segs):
    inputs, out = refs[:4], refs[4]
    buf_a, buf_b, table, sem = refs[5:]
    copy = pltpu.make_async_copy(packed, table, sem)
    copy.start()
    freq = lax.axis_index("freq")
    place = (freq >> (2 * stage)) & 3
    _, _, half_order, starts = stage_places(stage, section, freq)
    stride = ahead + segs
    for buf in (buf_a, buf_b):
        buf[...] = jnp.zeros(buf.shape, jnp.float32)
    rows = ROWS // 2 if local else ROWS
    in_segs = inputs[0].shape[0] // rows
    for by, ref in enumerate(inputs):
        to = (place ^ by) * (rows * stride) + ahead
        for row in range(rows):
            buf_a[pl.ds(to + row * stride, in_segs), :] = ref[pl.ds(row * in_segs, in_segs), :]
    copy.wait()
    src, dst = buf_a, buf_b

    def at_row(k):
        return k * stride + ahead

    for now in range(1, local):
        section_rows(src, dst, at_row, segs, 4 * ROWS, table, lambda k, now=now: (3 * (now - 1), k))
        src, dst = dst, src

    def mid_entry(k):
        band = k // ROWS
        if local:
            return 3 * (local - 1), 2 * ROWS * band + ROWS * half_order + k % ROWS
        return 3 * band, starts[band] % LANES + k % ROWS

    section_rows(src, dst, at_row, segs, 2 * ROWS, table, mid_entry)
    at = 3 * local if local else 6
    column = starts[2] % LANES
    section_rows(dst, out, lambda k: k * segs, segs, ROWS, table, lambda k: (at, column + k))


def final_kernel(packed, widths_all, *refs, stage, section, n_time, main_segs, trials, place_rows):
    own, moved = refs[:4], refs[4 : 3 + n_time]
    outs = refs[3 + n_time : 3 + 2 * n_time]
    buf, mid, data, edges, over, scale, table, widths, sems = refs[3 + 2 * n_time :]
    copies = [
        pltpu.make_async_copy(packed, table, sems.at[0]),
        pltpu.make_async_copy(widths_all, widths, sems.at[1]),
    ]
    for copy in copies:
        copy.start()
    freq = lax.axis_index("freq")
    tm = lax.axis_index("tm")
    place = (freq >> (2 * stage)) & 3
    first_trial = 4 * ROWS * order_of(freq, stage) + trials * tm
    _, _, _, starts = stage_places(stage, section, freq, first_trial)
    total_segs = n_time * main_segs
    total_time = total_segs * LANES
    stride = PAD + total_segs
    zeros = jnp.zeros((PAD, LANES), jnp.float32)
    for row in range(4 * ROWS):
        buf[pl.ds(row * stride, PAD), :] = zeros
    for row in range(2 * ROWS):
        mid[pl.ds(row * stride, PAD), :] = zeros
    in_segs = own[0].shape[0] // ROWS
    size = ROWS * in_segs
    sources = []
    for by_band in range(4):
        for by_time in range(n_time):
            start = (place ^ by_band) * (ROWS * stride) + PAD
            part = tm ^ by_time
            ref, at = (own[by_band], 0) if by_time == 0 else (moved[by_time - 1], by_band * size)
            sources.append((start, part, ref, at))
    for start, part, ref, at in sources:
        for row in range(ROWS):
            to = pl.multiple_of(start + part * main_segs + row * stride, 8)
            buf[pl.ds(to, main_segs), :] = ref[pl.ds(at + row * in_segs, main_segs), :]
    for start, part, ref, at in sources:
        to = start + jnp.minimum(part + 1, n_time - 1) * main_segs
        for seg in range(in_segs - main_segs):
            spill = ref[pl.ds(at + main_segs + seg, ROWS, stride=in_segs), :]
            where = pl.ds(to + seg, ROWS, stride=stride)
            buf[where, :] = buf[where, :] + jnp.where(part + 1 < n_time, spill, 0.0)
    for copy in copies:
        copy.wait()

    section_rows(
        buf,
        mid,
        lambda k: PAD + k * stride,
        total_segs,
        2 * ROWS,
        table,
        lambda k: (3 * (k // ROWS), starts[k // ROWS] % LANES + k % ROWS),
    )
    column = first_trial % LANES
    section_rows(mid, data, lambda k: k * total_segs, total_segs, trials, table, lambda k: (6, column + k))

    def samples(seg):
        return data[pl.ds(seg, trials, stride=total_segs), :]

    total = samples(0)
    for seg in range(1, total_segs):
        total = total + samples(seg)
    mean = jnp.sum(total, axis=1, keepdims=True) / total_time

    row_at = lax.broadcasted_iota(jnp.int32, (2 * LANES, LANES), 0)
    column_at = lax.broadcasted_iota(jnp.int32, (2 * LANES, LANES), 1)
    after = jnp.where(column_at > row_at, -1.0, 0.0)
    upto = jnp.where(column_at <= row_at - LANES, 1.0, 0.0)
    ones = jnp.where(row_at < LANES, after, upto).astype(jnp.bfloat16)
    ones = jnp.concatenate([ones] * 3, axis=1)
    squares = jnp.zeros((trials, LANES), jnp.float32)
    for seg in range(-1, main_segs):
        parts = []
        for part in range(n_time):
            at = part * main_segs + seg
            centred = samples(at) - mean if at >= 0 else jnp.zeros((trials, LANES), jnp.float32)
            if seg >= 0:
                squares = squares + centred * centred
            parts.append(centred)
        values = jnp.concatenate(parts, axis=0)
        terms = []
        for _ in range(3):
            term = values.astype(jnp.bfloat16)
            terms.append(term)
            values = values - term.astype(jnp.float32)
        both = lax.dot_general(
            ones,
            jnp.concatenate(terms, axis=1),
            (((1,), (1,)), ((), ())),
            preferred_element_type=jnp.float32,
        )
        if seg + 1 < main_segs:
            edges[pl.ds((seg + 1) * 2 * LANES, LANES), :] = both[:LANES]
        if seg >= 0:
            edges[pl.ds(seg * 2 * LANES + LANES, LANES), :] = both[LANES:]
    squares = jnp.sum(squares, axis=1, keepdims=True)
    inverse = 1.0 / jnp.sqrt(squares / total_time + eps_var)
    inverse = jnp.concatenate([jnp.broadcast_to(inverse, (trials, LANES))] * n_time, axis=0).T[:8]

    count = widths.shape[0]
    for j in range(count):
        scale[pl.ds(j * 8, 8), :] = jnp.full((8, LANES), widths[j], jnp.int32).astype(jnp.float32)
    scale[...] = 1.0 / jnp.sqrt(scale[...])
    tall = 64

    def spread_rows(value):
        return jnp.concatenate([value] * (tall // 8), axis=0)

    def fold(value):
        out = value[:8]
        for n in range(8, value.shape[0], 8):
            out = jnp.maximum(out, value[n : n + 8])
        return out

    peaks = jnp.full((8, LANES), -jnp.inf, jnp.float32)
    for seg in range(main_segs):
        blocks = []
        for first in range(0, LANES, tall):
            at = seg * 2 * LANES + LANES + first
            ends = edges[pl.ds(at, tall), :]
            best = None
            for j in range(count):
                score = (ends - edges[pl.ds(at - widths[j], tall), :]) * spread_rows(scale[pl.ds(j * 8, 8), :])
                best = score if j == 0 else jnp.maximum(best, score)
            best = best * spread_rows(inverse)
            peaks = jnp.maximum(peaks, fold(best))
            blocks.append(best)
        turned = jnp.concatenate(blocks, axis=0).T
        for part in range(n_time):
            over[pl.ds((part * main_segs + seg) * 8, 8), :] = fold(turned[part * trials : (part + 1) * trials])
    best_all = over[pl.ds(0, total_segs, stride=8), :]
    for n in range(1, 8):
        best_all = jnp.maximum(best_all, over[pl.ds(n, total_segs, stride=8), :])
    buf[pl.ds(0, total_segs), :] = best_all
    peak_row = jnp.max(peaks, axis=0, keepdims=True)
    step = trials
    while step < LANES:
        peak_row = jnp.maximum(peak_row, pltpu.roll(peak_row, step, axis=1))
        step *= 2
    offset = first_trial % LANES
    lane = lax.broadcasted_iota(jnp.int32, (1, LANES), 1)
    peak_row = jnp.where((lane >= offset) & (lane < offset + trials), peak_row, -jnp.inf)
    for by in range(n_time):
        at = pl.multiple_of((tm ^ by) * main_segs, 8)
        outs[by][pl.ds(0, main_segs), :] = buf[pl.ds(at, main_segs), :]
        outs[by][pl.ds(main_segs, place_rows), :] = jnp.full((place_rows, LANES), -jnp.inf, jnp.float32)
        outs[by][pl.ds(main_segs + first_trial // LANES, 1), :] = peak_row


def finish_kernel(*refs, main_segs, channels):
    inputs, (best_out, peaks_out), (best, row, peaks, sems) = refs[:-6], refs[-6:-4], refs[-4:]
    merged = inputs[0][...]
    for ref in inputs[1:]:
        merged = jnp.maximum(merged, ref[...])
    best[...] = merged[:main_segs]
    row[...] = merged[main_segs:]
    first = pltpu.make_async_copy(best, best_out, sems.at[0])
    first.start()
    start = lax.axis_index("freq") * channels
    mine = pltpu.roll(row[pl.ds(start // LANES, 1), :], (LANES - start % LANES) % LANES, axis=1)
    peaks[...] = mine[:, :channels]
    second = pltpu.make_async_copy(peaks, peaks_out, sems.at[1])
    second.start()
    first.wait()
    second.wait()


def call(kernel, name, inputs, out_shapes, scratch=(), tables=(), out_specs=VMEM, dtype=jnp.float32):
    outs = [jax.ShapeDtypeStruct(shape, dtype) for shape in out_shapes]
    used = sum(4 * v.size for v in inputs) + sum(4 * o.size for o in outs)
    used += sum(4 * s.shape[0] * s.shape[1] for s in scratch if len(s.shape) == 2)
    return pl.pallas_call(
        kernel,
        out_shape=outs,
        in_specs=[ANY] * len(tables) + [VMEM] * len(inputs),
        out_specs=[out_specs] * len(outs),
        scratch_shapes=list(scratch),
        compiler_params=pltpu.CompilerParams(vmem_limit_bytes=used + (2 << 20)),
        name=name,
    )(*tables, *inputs)


def floats(rows):
    return pltpu.VMEM((rows, LANES), jnp.float32)


def shards(spectra, lead_delay, tail_delay, widths):
    channels, span = spectra.shape
    n_freq = lax.axis_size("freq")
    n_time = lax.axis_size("tm")
    freq = lax.axis_index("freq")
    sections = lead_delay.shape[0]
    local = channels.bit_length() - 1
    stages = (n_freq.bit_length() - 1) // 2
    main_segs = span // LANES
    full_time = sections - 2

    def segs_after(stage):
        spill = sum(2**s - 1 for s in range(1, local + 2 * stage + 2))
        return main_segs + -(-spill // LANES)

    def ahead_of(stage):
        return 1 + ((2 ** (local + 2 * stage + 1) - 1) >> 7)

    pairs = channels // 2
    (current,) = call(
        pair_kernel,
        "pairs",
        [spectra],
        [(pairs * main_segs, LANES)],
        [floats(channels * main_segs)],
    )
    trials = 4 * ROWS // n_time
    total_segs = n_time * main_segs
    stride = PAD + total_segs
    strides = {}
    for section in range(1, sections):
        stage = max(0, section - local) // 2
        if section >= full_time:
            strides[section] = (stride, PAD)
        else:
            strides[section] = (ahead_of(stage) + segs_after(stage), ahead_of(stage))
    windows = 1 + 3 * (stages - 1)
    tables = call(
        functools.partial(
            tables_kernel, stages=stages, sections=sections, local=local, strides=strides, trials=trials
        ),
        "tables",
        [current],
        [(3 * (local + 1), LANES)] + [(9, LANES)] * (stages - 1),
        [pltpu.VMEM((windows, sections, LANES), jnp.int32)] * 2 + [pltpu.SemaphoreType.DMA((2 * windows,))],
        (lead_delay, tail_delay),
        dtype=jnp.int32,
    )
    for stage in range(stages - 1):
        section = local + 2 * stage
        others = [xor_permute(current, "freq", by << (2 * stage)) for by in (1, 2, 3)]
        ahead, segs = ahead_of(stage), segs_after(stage)
        (current,) = call(
            functools.partial(
                quad_kernel,
                stage=stage,
                section=section,
                local=local if stage == 0 else 0,
                ahead=ahead,
                segs=segs,
            ),
            "quad",
            [current, *others],
            [(ROWS * segs, LANES)],
            [
                floats(4 * ROWS * (ahead + segs)),
                floats(4 * ROWS * (ahead + segs)),
                pltpu.SMEM(tables[stage].shape, jnp.int32),
                pltpu.SemaphoreType.DMA(()),
            ],
            [tables[stage]],
        )
    stage = stages - 1
    two = xor_permute(current, "freq", 2 << (2 * stage))
    one = xor_permute(current, "freq", 1 << (2 * stage))
    three = xor_permute(two, "freq", 1 << (2 * stage))
    bands = [current, one, two, three]
    stacked = jnp.concatenate(bands, axis=0)
    arrays = bands + [xor_permute(stacked, "tm", by) for by in range(1, n_time)]
    peak_rows = channels * n_freq // LANES
    place_rows = -(-peak_rows // 8) * 8
    pieces = call(
        functools.partial(
            final_kernel,
            stage=stage,
            section=full_time,
            n_time=n_time,
            main_segs=main_segs,
            trials=trials,
            place_rows=place_rows,
        ),
        "final",
        arrays,
        [(main_segs + place_rows, LANES)] * n_time,
        [
            floats(4 * ROWS * stride),
            floats(2 * ROWS * stride),
            floats(trials * total_segs),
            floats(2 * LANES * main_segs),
            floats(8 * total_segs),
            floats(widths.shape[0] * 8),
            pltpu.SMEM(tables[stage].shape, jnp.int32),
            pltpu.SMEM(widths.shape, jnp.int32),
            pltpu.SemaphoreType.DMA((2,)),
        ],
        [tables[stage], widths],
    )
    merged = pieces[0]
    for by in range(1, n_time):
        merged = jnp.maximum(merged, xor_permute(pieces[by], "tm", by))
    for stage in range(stages - 1):
        received = [merged] + [xor_permute(merged, "freq", by << (2 * stage)) for by in (1, 2, 3)]
        if stage < stages - 2:
            merged = functools.reduce(jnp.maximum, received)
    best_snr, trial_peak = call(
        functools.partial(finish_kernel, main_segs=main_segs, channels=channels),
        "finish",
        received,
        [(main_segs, LANES), (1, channels)],
        [
            floats(main_segs),
            floats(place_rows),
            pltpu.VMEM((1, channels), jnp.float32),
            pltpu.SemaphoreType.DMA((2,)),
        ],
        out_specs=ANY,
    )
    return (best_snr.reshape(span), trial_peak.reshape(channels))


def solution(mesh):
    placed = (P("freq", "tm"), P(), P(), P())
    return jax.shard_map(
        shards, mesh=mesh, in_specs=placed, out_specs=(P("tm"), P("freq")), check_vma=False
    )
```

```python
import functools
import math

import jax
import jax.numpy as jnp
from jax import lax
from jax.experimental import pallas as pl
from jax.experimental.pallas import tpu as pltpu
from jax.sharding import PartitionSpec as P

LANES = 128
ROWS = 32
PAD = 8

eps_var = 1e-06
VMEM = pl.BlockSpec(memory_space=pltpu.VMEM)
ANY = pl.BlockSpec(memory_space=pl.ANY)
SMEM = pl.BlockSpec(memory_space=pltpu.SMEM)


def xor_permute(value, axis, by):
    return lax.ppermute(value, axis, [(i, i ^ by) for i in range(lax.axis_size(axis))])


def section_rows(src, dst, dst_row, segs, rows, table, entry, group=16):
    lane = lax.broadcasted_iota(jnp.int32, (segs, LANES), 1)
    for first in range(0, rows, group):
        picked = []
        for k in range(first, min(first + group, rows)):
            at, column = entry(k)
            start, delay = table[at + 1, column], table[at + 2, column]
            lower = src[pl.ds(table[at, column], segs), :]
            picked.append((k, delay, lower, src[pl.ds(start, segs), :], src[pl.ds(start - 1, segs), :]))
        for k, delay, lower, here, before in picked:
            mixed = jnp.where(lane < LANES - delay, here, before)
            dst[pl.ds(dst_row(k), segs), :] = lower + pltpu.roll(mixed, delay, axis=1)


def window(start):
    return pl.multiple_of((start // LANES) * LANES, LANES)


def order_of(freq, stage):
    order = 0
    for n in range(stage):
        order = 4 * order + ((freq >> (2 * n)) & 3)
    return order


def pair_kernel(x, out, stage):
    channels, span = x.shape
    segs = span // LANES
    half = channels // 2
    for seg in range(segs):
        stage[pl.ds(seg * channels, channels), :] = x[:, pl.ds(seg * LANES, LANES)]
    for seg in range(segs):
        first = seg * channels
        summed = stage[pl.ds(first, half, stride=2), :] + stage[pl.ds(first + 1, half, stride=2), :]
        out[pl.ds(seg, half, stride=segs), :] = summed


def stage_places(stage, section, freq, trials_first=None):
    order = order_of(freq, stage)
    place = (freq >> (2 * stage)) & 3
    rows_in = 2**section
    base = (freq >> (2 * stage + 2)) * (4 * rows_in)
    last = base + ROWS * (4 * order + place) if trials_first is None else trials_first
    half_order = (last - base) // (2 * ROWS)
    starts = [base + ROWS * half_order, base + 2 * rows_in + ROWS * half_order, last]
    return base, order, half_order, starts


def tables_kernel(lead_all, tail_all, widths_all, order_after, *refs, stages, sections, local, strides, trials):
    del order_after
    finals, widths = refs[:stages], refs[stages]
    outs, (lead, tail, sems) = refs[stages + 1 : 2 * stages + 1], refs[2 * stages + 1 :]
    freq = lax.axis_index("freq")
    plans = []
    for stage in range(stages):
        section = local + 2 * stage
        first_trial = None
        if stage == stages - 1:
            first_trial = 4 * ROWS * order_of(freq, stage) + trials * lax.axis_index("tm")
        base, order, half_order, starts = stage_places(stage, section, freq, first_trial)
        plans.append((section, order, half_order, [base] if stage == 0 else starts))
    copies = []
    slot = 0
    for *_, wheres in plans:
        for where in wheres:
            for table, to in ((lead_all, lead), (tail_all, tail)):
                part = table.at[:, pl.ds(window(where), LANES)]
                copies.append(pltpu.make_async_copy(part, to.at[slot], sems.at[len(copies)]))
            slot += 1
    copies.append(pltpu.make_async_copy(widths_all, widths, sems.at[len(copies)]))
    for copy in copies:
        copy.start()
    for copy in copies:
        copy.wait()
    lane = lax.broadcasted_iota(jnp.int32, (1, LANES), 1)
    slot = 0
    for stage, (section, order, half_order, wheres) in enumerate(plans):
        out, at = outs[stage], 0
        jobs = []
        if stage == 0:
            for now in range(1, local):
                band = lane // (2 * 2**now)
                rows = (2 * band, 2 * band + 1) if now == 1 else (2 * band * 2**now, (2 * band + 1) * 2**now)
                jobs.append((slot, now, *rows, now > 1, strides[now]))
            band = lane // (2 * ROWS)
            jobs.append((slot, section, 2 * band * ROWS, (2 * band + 1) * ROWS, True, strides[section]))
            jobs.append((slot, section + 1, -ROWS * half_order, ROWS - ROWS * half_order, True, strides[section + 1]))
        else:
            for band in range(2):
                low = 2 * band * ROWS - ROWS * order
                jobs.append((slot + band, section, low, low + ROWS, True, strides[section]))
            low = -ROWS * half_order
            jobs.append((slot + 2, section + 1, low, low + ROWS, True, strides[section + 1]))
        for where, row, low, up, picks, (stride, ahead) in jobs:
            e, h = lead[where, pl.ds(row, 1), :], tail[where, pl.ds(row, 1), :]
            out[pl.ds(at, 1), :] = (low + e if picks else low) * stride + ahead
            out[pl.ds(at + 1, 1), :] = (up + h if picks else up) * stride + ahead - (e >> 7)
            out[pl.ds(at + 2, 1), :] = e & (LANES - 1)
            at += 3
        slot += len(wheres)
    copies = [pltpu.make_async_copy(outs[n], finals[n], sems.at[n]) for n in range(stages)]
    for copy in copies:
        copy.start()
    for copy in copies:
        copy.wait()


def quad_kernel(table, *refs, stage, section, local, ahead, segs):
    inputs, out = refs[:4], refs[4]
    buf_a, buf_b = refs[5:]
    freq = lax.axis_index("freq")
    place = (freq >> (2 * stage)) & 3
    _, _, half_order, starts = stage_places(stage, section, freq)
    stride = ahead + segs
    for buf in (buf_a, buf_b):
        buf[...] = jnp.zeros(buf.shape, jnp.float32)
    rows = ROWS // 2 if local else ROWS
    in_segs = inputs[0].shape[0] // rows
    for by, ref in enumerate(inputs):
        to = (place ^ by) * (rows * stride) + ahead
        for row in range(rows):
            buf_a[pl.ds(to + row * stride, in_segs), :] = ref[pl.ds(row * in_segs, in_segs), :]
    src, dst = buf_a, buf_b

    def at_row(k):
        return k * stride + ahead

    for now in range(1, local):
        section_rows(src, dst, at_row, segs, 4 * ROWS, table, lambda k, now=now: (3 * (now - 1), k))
        src, dst = dst, src

    def mid_entry(k):
        band = k // ROWS
        if local:
            return 3 * (local - 1), 2 * ROWS * band + ROWS * half_order + k % ROWS
        return 3 * band, starts[band] % LANES + k % ROWS

    section_rows(src, dst, at_row, segs, 2 * ROWS, table, mid_entry)
    at = 3 * local if local else 6
    column = starts[2] % LANES
    section_rows(dst, out, lambda k: k * segs, segs, ROWS, table, lambda k: (at, column + k))


def final_kernel(table, widths, *refs, stage, section, n_time, main_segs, trials, place_rows):
    own, moved = refs[:4], refs[4 : 3 + n_time]
    outs = refs[3 + n_time : 3 + 2 * n_time]
    buf, mid, data, edges, over, scale = refs[3 + 2 * n_time :]
    freq = lax.axis_index("freq")
    tm = lax.axis_index("tm")
    place = (freq >> (2 * stage)) & 3
    first_trial = 4 * ROWS * order_of(freq, stage) + trials * tm
    _, _, _, starts = stage_places(stage, section, freq, first_trial)
    total_segs = n_time * main_segs
    total_time = total_segs * LANES
    stride = PAD + total_segs
    zeros = jnp.zeros((PAD, LANES), jnp.float32)
    for row in range(4 * ROWS):
        buf[pl.ds(row * stride, PAD), :] = zeros
    for row in range(2 * ROWS):
        mid[pl.ds(row * stride, PAD), :] = zeros
    in_segs = own[0].shape[0] // ROWS
    size = ROWS * in_segs
    sources = []
    for by_band in range(4):
        for by_time in range(n_time):
            start = (place ^ by_band) * (ROWS * stride) + PAD
            part = tm ^ by_time
            ref, at = (own[by_band], 0) if by_time == 0 else (moved[by_time - 1], by_band * size)
            sources.append((start, part, ref, at))
    for start, part, ref, at in sources:
        for row in range(ROWS):
            to = pl.multiple_of(start + part * main_segs + row * stride, 8)
            buf[pl.ds(to, main_segs), :] = ref[pl.ds(at + row * in_segs, main_segs), :]
    for start, part, ref, at in sources:
        to = start + jnp.minimum(part + 1, n_time - 1) * main_segs
        for seg in range(in_segs - main_segs):
            spill = ref[pl.ds(at + main_segs + seg, ROWS, stride=in_segs), :]
            where = pl.ds(to + seg, ROWS, stride=stride)
            buf[where, :] = buf[where, :] + jnp.where(part + 1 < n_time, spill, 0.0)

    section_rows(
        buf,
        mid,
        lambda k: PAD + k * stride,
        total_segs,
        2 * ROWS,
        table,
        lambda k: (3 * (k // ROWS), starts[k // ROWS] % LANES + k % ROWS),
    )
    column = first_trial % LANES
    section_rows(mid, data, lambda k: k * total_segs, total_segs, trials, table, lambda k: (6, column + k))

    def samples(seg):
        return data[pl.ds(seg, trials, stride=total_segs), :]

    total = samples(0)
    for seg in range(1, total_segs):
        total = total + samples(seg)
    mean = jnp.sum(total, axis=1, keepdims=True) / total_time

    row_at = lax.broadcasted_iota(jnp.int32, (2 * LANES, LANES), 0)
    column_at = lax.broadcasted_iota(jnp.int32, (2 * LANES, LANES), 1)
    after = jnp.where(column_at > row_at, -1.0, 0.0)
    upto = jnp.where(column_at <= row_at - LANES, 1.0, 0.0)
    ones = jnp.where(row_at < LANES, after, upto).astype(jnp.bfloat16)
    ones = jnp.concatenate([ones] * 3, axis=1)
    squares = jnp.zeros((trials, LANES), jnp.float32)
    for seg in range(-1, main_segs):
        parts = []
        for part in range(n_time):
            at = part * main_segs + seg
            centred = samples(at) - mean if at >= 0 else jnp.zeros((trials, LANES), jnp.float32)
            if seg >= 0:
                squares = squares + centred * centred
            parts.append(centred)
        values = jnp.concatenate(parts, axis=0)
        terms = []
        for _ in range(3):
            term = values.astype(jnp.bfloat16)
            terms.append(term)
            values = values - term.astype(jnp.float32)
        both = lax.dot_general(
            ones,
            jnp.concatenate(terms, axis=1),
            (((1,), (1,)), ((), ())),
            preferred_element_type=jnp.float32,
        )
        if seg + 1 < main_segs:
            edges[pl.ds((seg + 1) * 2 * LANES, LANES), :] = both[:LANES]
        if seg >= 0:
            edges[pl.ds(seg * 2 * LANES + LANES, LANES), :] = both[LANES:]
    squares = jnp.sum(squares, axis=1, keepdims=True)
    inverse = 1.0 / jnp.sqrt(squares / total_time + eps_var)
    inverse = jnp.concatenate([jnp.broadcast_to(inverse, (trials, LANES))] * n_time, axis=0).T[:8]

    count = widths.shape[0]
    for j in range(count):
        scale[pl.ds(j * 8, 8), :] = jnp.full((8, LANES), widths[j], jnp.int32).astype(jnp.float32)
    scale[...] = 1.0 / jnp.sqrt(scale[...])
    tall = 64

    def spread_rows(value):
        return jnp.concatenate([value] * (tall // 8), axis=0)

    def fold(value):
        out = value[:8]
        for n in range(8, value.shape[0], 8):
            out = jnp.maximum(out, value[n : n + 8])
        return out

    peaks = jnp.full((8, LANES), -jnp.inf, jnp.float32)
    for seg in range(main_segs):
        blocks = []
        for first in range(0, LANES, tall):
            at = seg * 2 * LANES + LANES + first
            ends = edges[pl.ds(at, tall), :]
            best = None
            for j in range(count):
                score = (ends - edges[pl.ds(at - widths[j], tall), :]) * spread_rows(scale[pl.ds(j * 8, 8), :])
                best = score if j == 0 else jnp.maximum(best, score)
            best = best * spread_rows(inverse)
            peaks = jnp.maximum(peaks, fold(best))
            blocks.append(best)
        turned = jnp.concatenate(blocks, axis=0).T
        for part in range(n_time):
            over[pl.ds((part * main_segs + seg) * 8, 8), :] = fold(turned[part * trials : (part + 1) * trials])
    best_all = over[pl.ds(0, total_segs, stride=8), :]
    for n in range(1, 8):
        best_all = jnp.maximum(best_all, over[pl.ds(n, total_segs, stride=8), :])
    buf[pl.ds(0, total_segs), :] = best_all
    peak_row = jnp.max(peaks, axis=0, keepdims=True)
    step = trials
    while step < LANES:
        peak_row = jnp.maximum(peak_row, pltpu.roll(peak_row, step, axis=1))
        step *= 2
    offset = first_trial % LANES
    lane = lax.broadcasted_iota(jnp.int32, (1, LANES), 1)
    peak_row = jnp.where((lane >= offset) & (lane < offset + trials), peak_row, -jnp.inf)
    for by in range(n_time):
        at = pl.multiple_of((tm ^ by) * main_segs, 8)
        outs[by][pl.ds(0, main_segs), :] = buf[pl.ds(at, main_segs), :]
        outs[by][pl.ds(main_segs, place_rows), :] = jnp.full((place_rows, LANES), -jnp.inf, jnp.float32)
        outs[by][pl.ds(main_segs + first_trial // LANES, 1), :] = peak_row


def finish_kernel(*refs, main_segs, channels):
    inputs, (best_out, peaks_out), (best, row, peaks, sems) = refs[:-6], refs[-6:-4], refs[-4:]
    merged = inputs[0][...]
    for ref in inputs[1:]:
        merged = jnp.maximum(merged, ref[...])
    best[...] = merged[:main_segs]
    row[...] = merged[main_segs:]
    first = pltpu.make_async_copy(best, best_out, sems.at[0])
    first.start()
    start = lax.axis_index("freq") * channels
    mine = pltpu.roll(row[pl.ds(start // LANES, 1), :], (LANES - start % LANES) % LANES, axis=1)
    peaks[...] = mine[:, :channels]
    second = pltpu.make_async_copy(peaks, peaks_out, sems.at[1])
    second.start()
    first.wait()
    second.wait()


def call(kernel, name, inputs, outs, scratch=(), tables=(), table_specs=SMEM, out_specs=VMEM):
    outs = [jax.ShapeDtypeStruct(out, jnp.float32) if isinstance(out, tuple) else out for out in outs]
    used = sum(4 * v.size for v in inputs) + sum(4 * math.prod(o.shape) for o in outs)
    used += sum(4 * math.prod(s.shape) for s in scratch)
    return pl.pallas_call(
        kernel,
        out_shape=outs,
        in_specs=[table_specs] * len(tables) + [VMEM] * len(inputs),
        out_specs=[out_specs] * len(outs),
        scratch_shapes=list(scratch),
        compiler_params=pltpu.CompilerParams(vmem_limit_bytes=used + (2 << 20)),
        name=name,
    )(*tables, *inputs)


def floats(rows):
    return pltpu.VMEM((rows, LANES), jnp.float32)


def shards(spectra, lead_delay, tail_delay, widths):
    channels, span = spectra.shape
    n_freq = lax.axis_size("freq")
    n_time = lax.axis_size("tm")
    freq = lax.axis_index("freq")
    sections = lead_delay.shape[0]
    local = channels.bit_length() - 1
    stages = (n_freq.bit_length() - 1) // 2
    main_segs = span // LANES
    full_time = sections - 2

    def segs_after(stage):
        spill = sum(2**s - 1 for s in range(1, local + 2 * stage + 2))
        return main_segs + -(-spill // LANES)

    def ahead_of(stage):
        return 1 + ((2 ** (local + 2 * stage + 1) - 1) >> 7)

    pairs = channels // 2
    (current,) = call(
        pair_kernel,
        "pairs",
        [spectra],
        [(pairs * main_segs, LANES)],
        [floats(channels * main_segs)],
    )
    trials = 4 * ROWS // n_time
    total_segs = n_time * main_segs
    stride = PAD + total_segs
    strides = {}
    for section in range(1, sections):
        stage = max(0, section - local) // 2
        if section >= full_time:
            strides[section] = (stride, PAD)
        else:
            strides[section] = (ahead_of(stage) + segs_after(stage), ahead_of(stage))
    windows = 1 + 3 * (stages - 1)
    shapes = [(3 * (local + 1), LANES)] + [(9, LANES)] * (stages - 1)
    *tables, widths = call(
        functools.partial(
            tables_kernel, stages=stages, sections=sections, local=local, strides=strides, trials=trials
        ),
        "tables",
        [current],
        [pltpu.SMEM(shape, jnp.int32) for shape in [*shapes, widths.shape]],
        [
            *[pltpu.VMEM(shape, jnp.int32) for shape in shapes],
            *[pltpu.VMEM((windows, sections, LANES), jnp.int32)] * 2,
            pltpu.SemaphoreType.DMA((2 * windows + 1,)),
        ],
        (lead_delay, tail_delay, widths),
        table_specs=ANY,
        out_specs=SMEM,
    )
    for stage in range(stages - 1):
        section = local + 2 * stage
        others = [xor_permute(current, "freq", by << (2 * stage)) for by in (1, 2, 3)]
        ahead, segs = ahead_of(stage), segs_after(stage)
        (current,) = call(
            functools.partial(
                quad_kernel,
                stage=stage,
                section=section,
                local=local if stage == 0 else 0,
                ahead=ahead,
                segs=segs,
            ),
            "quad",
            [current, *others],
            [(ROWS * segs, LANES)],
            [
                floats(4 * ROWS * (ahead + segs)),
                floats(4 * ROWS * (ahead + segs)),
            ],
            [tables[stage]],
        )
    stage = stages - 1
    two = xor_permute(current, "freq", 2 << (2 * stage))
    one = xor_permute(current, "freq", 1 << (2 * stage))
    three = xor_permute(two, "freq", 1 << (2 * stage))
    bands = [current, one, two, three]
    stacked = jnp.concatenate(bands, axis=0)
    arrays = bands + [xor_permute(stacked, "tm", by) for by in range(1, n_time)]
    peak_rows = channels * n_freq // LANES
    place_rows = -(-peak_rows // 8) * 8
    pieces = call(
        functools.partial(
            final_kernel,
            stage=stage,
            section=full_time,
            n_time=n_time,
            main_segs=main_segs,
            trials=trials,
            place_rows=place_rows,
        ),
        "final",
        arrays,
        [(main_segs + place_rows, LANES)] * n_time,
        [
            floats(4 * ROWS * stride),
            floats(2 * ROWS * stride),
            floats(trials * total_segs),
            floats(2 * LANES * main_segs),
            floats(8 * total_segs),
            floats(widths.shape[0] * 8),
        ],
        [tables[stage], widths],
    )
    merged = pieces[0]
    for by in range(1, n_time):
        merged = jnp.maximum(merged, xor_permute(pieces[by], "tm", by))
    for stage in range(stages - 1):
        received = [merged] + [xor_permute(merged, "freq", by << (2 * stage)) for by in (1, 2, 3)]
        if stage < stages - 2:
            merged = functools.reduce(jnp.maximum, received)
    best_snr, trial_peak = call(
        functools.partial(finish_kernel, main_segs=main_segs, channels=channels),
        "finish",
        received,
        [(main_segs, LANES), (1, channels)],
        [
            floats(main_segs),
            floats(place_rows),
            pltpu.VMEM((1, channels), jnp.float32),
            pltpu.SemaphoreType.DMA((2,)),
        ],
        out_specs=ANY,
    )
    return (best_snr.reshape(span), trial_peak.reshape(channels))


def solution(mesh):
    placed = (P("freq", "tm"), P(), P(), P())
    return jax.shard_map(
        shards, mesh=mesh, in_specs=placed, out_specs=(P("tm"), P("freq")), check_vma=False
    )
```

```python
import functools
import math

import jax
import jax.numpy as jnp
from jax import lax
from jax.experimental import pallas as pl
from jax.experimental.pallas import tpu as pltpu
from jax.sharding import PartitionSpec as P

LANES = 128
ROWS = 32
PAD = 8

eps_var = 1e-06
VMEM = pl.BlockSpec(memory_space=pltpu.VMEM)
ANY = pl.BlockSpec(memory_space=pl.ANY)
SMEM = pl.BlockSpec(memory_space=pltpu.SMEM)


def xor_permute(value, axis, by):
    return lax.ppermute(value, axis, [(i, i ^ by) for i in range(lax.axis_size(axis))])


def section_rows(src, dst, dst_row, segs, rows, table, entry, group=16):
    lane = lax.broadcasted_iota(jnp.int32, (segs, LANES), 1)
    for first in range(0, rows, group):
        picked = []
        for k in range(first, min(first + group, rows)):
            at, column = entry(k)
            start, delay = table[at + 1, column], table[at + 2, column]
            lower = src[pl.ds(table[at, column], segs), :]
            picked.append((k, delay, lower, src[pl.ds(start, segs), :], src[pl.ds(start - 1, segs), :]))
        for k, delay, lower, here, before in picked:
            mixed = jnp.where(lane < LANES - delay, here, before)
            dst[pl.ds(dst_row(k), segs), :] = lower + pltpu.roll(mixed, delay, axis=1)


def window(start):
    return pl.multiple_of((start // LANES) * LANES, LANES)


def order_of(freq, stage):
    order = 0
    for n in range(stage):
        order = 4 * order + ((freq >> (2 * n)) & 3)
    return order


def pair_kernel(x, out, stage):
    channels, span = x.shape
    segs = span // LANES
    half = channels // 2
    for seg in range(segs):
        stage[pl.ds(seg * channels, channels), :] = x[:, pl.ds(seg * LANES, LANES)]
    for seg in range(segs):
        first = seg * channels
        summed = stage[pl.ds(first, half, stride=2), :] + stage[pl.ds(first + 1, half, stride=2), :]
        out[pl.ds(seg, half, stride=segs), :] = summed


def stage_places(stage, section, freq, trials_first=None):
    order = order_of(freq, stage)
    place = (freq >> (2 * stage)) & 3
    rows_in = 2**section
    base = (freq >> (2 * stage + 2)) * (4 * rows_in)
    last = base + ROWS * (4 * order + place) if trials_first is None else trials_first
    half_order = (last - base) // (2 * ROWS)
    starts = [base + ROWS * half_order, base + 2 * rows_in + ROWS * half_order, last]
    return base, order, half_order, starts


def tables_kernel(lead_all, tail_all, widths_all, order_after, *refs, stages, sections, local, strides, trials):
    del order_after
    finals, widths = refs[:stages], refs[stages]
    outs, (lead, tail, sems) = refs[stages + 1 : 2 * stages + 1], refs[2 * stages + 1 :]
    freq = lax.axis_index("freq")
    plans = []
    for stage in range(stages):
        section = local + 2 * stage
        first_trial = None
        if stage == stages - 1:
            first_trial = 4 * ROWS * order_of(freq, stage) + trials * lax.axis_index("tm")
        base, order, half_order, starts = stage_places(stage, section, freq, first_trial)
        plans.append((section, order, half_order, [base] if stage == 0 else starts))
    copies = []
    slot = 0
    for *_, wheres in plans:
        for where in wheres:
            for table, to in ((lead_all, lead), (tail_all, tail)):
                part = table.at[:, pl.ds(window(where), LANES)]
                copies.append(pltpu.make_async_copy(part, to.at[slot], sems.at[len(copies)]))
            slot += 1
    copies.append(pltpu.make_async_copy(widths_all, widths, sems.at[len(copies)]))
    for copy in copies:
        copy.start()
    for copy in copies:
        copy.wait()
    lane = lax.broadcasted_iota(jnp.int32, (1, LANES), 1)

    def by_distance(value):
        for bit, width in enumerate((ROWS, 2 * ROWS)):
            ahead = pltpu.roll(value, LANES - width, axis=1)
            swapped = jnp.where((lane // width) % 2 == 0, ahead, pltpu.roll(value, width, axis=1))
            value = jnp.where(((freq >> bit) & 1) == 1, swapped, value)
        return value

    slot = 0
    for stage, (section, order, half_order, wheres) in enumerate(plans):
        out, at = outs[stage], 0
        jobs = []
        if stage == 0:
            for now in range(1, local):
                band = lane // (2 * 2**now)
                rows = (2 * band, 2 * band + 1) if now == 1 else (2 * band * 2**now, (2 * band + 1) * 2**now)
                jobs.append((slot, now, *rows, now > 1, strides[now]))
            band = lane // (2 * ROWS)
            place = freq & 3
            rows = ((2 * band) ^ place) * ROWS, ((2 * band + 1) ^ place) * ROWS
            jobs.append((slot, section, *rows, True, strides[section]))
            jobs.append((slot, section + 1, -ROWS * half_order, ROWS - ROWS * half_order, True, strides[section + 1]))
        else:
            for band in range(2):
                low = 2 * band * ROWS - ROWS * order
                jobs.append((slot + band, section, low, low + ROWS, True, strides[section]))
            low = -ROWS * half_order
            jobs.append((slot + 2, section + 1, low, low + ROWS, True, strides[section + 1]))
        for where, row, low, up, picks, (stride, ahead) in jobs:
            e, h = lead[where, pl.ds(row, 1), :], tail[where, pl.ds(row, 1), :]
            if row < section:
                e, h = by_distance(e), by_distance(h)
            out[pl.ds(at, 1), :] = (low + e if picks else low) * stride + ahead
            out[pl.ds(at + 1, 1), :] = (up + h if picks else up) * stride + ahead - (e >> 7)
            out[pl.ds(at + 2, 1), :] = e & (LANES - 1)
            at += 3
        slot += len(wheres)
    copies = [pltpu.make_async_copy(outs[n], finals[n], sems.at[n]) for n in range(stages)]
    for copy in copies:
        copy.start()
    for copy in copies:
        copy.wait()


def local_sections(table, pieces, buf_a, buf_b, local, ahead, segs, out=None):
    stride = ahead + segs
    half = ROWS // 2
    for buf in (buf_a, buf_b):
        buf[...] = jnp.zeros(buf.shape, jnp.float32)
    for by, ref in pieces:
        in_segs = ref.shape[0] // half
        to = by * (half * stride) + ahead
        for row in range(half):
            buf_a[pl.ds(to + row * stride, in_segs), :] = ref[pl.ds(row * in_segs, in_segs), :]
    src, dst = buf_a, buf_b
    for now in range(1, local):
        to_out = out is not None and now == local - 1
        for n, (by, _) in enumerate(pieces):
            base = by * ROWS
            first, step = (n * ROWS * segs, segs) if to_out else (base * stride + ahead, stride)
            section_rows(
                src,
                out if to_out else dst,
                lambda k, first=first, step=step: first + k * step,
                segs,
                ROWS,
                table,
                lambda k, now=now, base=base: (3 * (now - 1), base + k),
            )
        src, dst = dst, src
    return src, dst


def early_kernel(table, own, two, three, out, buf_a, buf_b, *, local, ahead, segs):
    local_sections(table, [(0, own), (2, two), (3, three)], buf_a, buf_b, local, ahead, segs, out)


def quad_kernel(table, *refs, stage, section, local, ahead, segs):
    *inputs, out, buf_a, buf_b = refs
    freq = lax.axis_index("freq")
    place = (freq >> (2 * stage)) & 3
    _, _, half_order, starts = stage_places(stage, section, freq)
    stride = ahead + segs

    def at_row(k):
        return k * stride + ahead

    if local:
        early, late = inputs
        src, dst = local_sections(table, [(1, late)], buf_a, buf_b, local, ahead, segs)
        ready = [(by, early, n * ROWS * segs, segs) for n, by in enumerate((0, 2, 3))]
    else:
        src, dst = buf_a, buf_b
        for buf in (buf_a, buf_b):
            buf[...] = jnp.zeros(buf.shape, jnp.float32)
        ready = [(by, ref, 0, ref.shape[0] // ROWS) for by, ref in enumerate(inputs)]
    for by, ref, at, in_segs in ready:
        to = (by if local else place ^ by) * (ROWS * stride) + ahead
        for row in range(ROWS):
            src[pl.ds(to + row * stride, in_segs), :] = ref[pl.ds(at + row * in_segs, in_segs), :]

    def mid_entry(k):
        band = k // ROWS
        if local:
            return 3 * (local - 1), 2 * ROWS * band + ROWS * half_order + k % ROWS
        return 3 * band, starts[band] % LANES + k % ROWS

    section_rows(src, dst, at_row, segs, 2 * ROWS, table, mid_entry)
    at = 3 * local if local else 6
    column = starts[2] % LANES
    section_rows(dst, out, lambda k: k * segs, segs, ROWS, table, lambda k: (at, column + k))


def final_kernel(table, widths, *refs, stage, section, n_time, main_segs, trials, place_rows):
    own, moved = refs[:4], refs[4 : 3 + n_time]
    outs = refs[3 + n_time : 3 + 2 * n_time]
    buf, mid, data, edges, over, scale = refs[3 + 2 * n_time :]
    freq = lax.axis_index("freq")
    tm = lax.axis_index("tm")
    place = (freq >> (2 * stage)) & 3
    first_trial = 4 * ROWS * order_of(freq, stage) + trials * tm
    _, _, _, starts = stage_places(stage, section, freq, first_trial)
    total_segs = n_time * main_segs
    total_time = total_segs * LANES
    stride = PAD + total_segs
    zeros = jnp.zeros((PAD, LANES), jnp.float32)
    for row in range(4 * ROWS):
        buf[pl.ds(row * stride, PAD), :] = zeros
    for row in range(2 * ROWS):
        mid[pl.ds(row * stride, PAD), :] = zeros
    in_segs = own[0].shape[0] // ROWS
    size = ROWS * in_segs
    sources = []
    for by_band in range(4):
        for by_time in range(n_time):
            start = (place ^ by_band) * (ROWS * stride) + PAD
            part = tm ^ by_time
            ref, at = (own[by_band], 0) if by_time == 0 else (moved[by_time - 1], by_band * size)
            sources.append((start, part, ref, at))
    for start, part, ref, at in sources:
        for row in range(ROWS):
            to = pl.multiple_of(start + part * main_segs + row * stride, 8)
            buf[pl.ds(to, main_segs), :] = ref[pl.ds(at + row * in_segs, main_segs), :]
    for start, part, ref, at in sources:
        to = start + jnp.minimum(part + 1, n_time - 1) * main_segs
        for seg in range(in_segs - main_segs):
            spill = ref[pl.ds(at + main_segs + seg, ROWS, stride=in_segs), :]
            where = pl.ds(to + seg, ROWS, stride=stride)
            buf[where, :] = buf[where, :] + jnp.where(part + 1 < n_time, spill, 0.0)

    section_rows(
        buf,
        mid,
        lambda k: PAD + k * stride,
        total_segs,
        2 * ROWS,
        table,
        lambda k: (3 * (k // ROWS), starts[k // ROWS] % LANES + k % ROWS),
    )
    column = first_trial % LANES
    section_rows(mid, data, lambda k: k * total_segs, total_segs, trials, table, lambda k: (6, column + k))

    def samples(seg):
        return data[pl.ds(seg, trials, stride=total_segs), :]

    total = samples(0)
    for seg in range(1, total_segs):
        total = total + samples(seg)
    mean = jnp.sum(total, axis=1, keepdims=True) / total_time

    row_at = lax.broadcasted_iota(jnp.int32, (2 * LANES, LANES), 0)
    column_at = lax.broadcasted_iota(jnp.int32, (2 * LANES, LANES), 1)
    after = jnp.where(column_at > row_at, -1.0, 0.0)
    upto = jnp.where(column_at <= row_at - LANES, 1.0, 0.0)
    ones = jnp.where(row_at < LANES, after, upto).astype(jnp.bfloat16)
    ones = jnp.concatenate([ones] * 3, axis=1)
    squares = jnp.zeros((trials, LANES), jnp.float32)
    for seg in range(-1, main_segs):
        parts = []
        for part in range(n_time):
            at = part * main_segs + seg
            centred = samples(at) - mean if at >= 0 else jnp.zeros((trials, LANES), jnp.float32)
            if seg >= 0:
                squares = squares + centred * centred
            parts.append(centred)
        values = jnp.concatenate(parts, axis=0)
        terms = []
        for _ in range(3):
            term = values.astype(jnp.bfloat16)
            terms.append(term)
            values = values - term.astype(jnp.float32)
        both = lax.dot_general(
            ones,
            jnp.concatenate(terms, axis=1),
            (((1,), (1,)), ((), ())),
            preferred_element_type=jnp.float32,
        )
        if seg + 1 < main_segs:
            edges[pl.ds((seg + 1) * 2 * LANES, LANES), :] = both[:LANES]
        if seg >= 0:
            edges[pl.ds(seg * 2 * LANES + LANES, LANES), :] = both[LANES:]
    squares = jnp.sum(squares, axis=1, keepdims=True)
    inverse = 1.0 / jnp.sqrt(squares / total_time + eps_var)
    inverse = jnp.concatenate([jnp.broadcast_to(inverse, (trials, LANES))] * n_time, axis=0).T[:8]

    count = widths.shape[0]
    for j in range(count):
        scale[pl.ds(j * 8, 8), :] = jnp.full((8, LANES), widths[j], jnp.int32).astype(jnp.float32)
    scale[...] = 1.0 / jnp.sqrt(scale[...])
    tall = 64

    def spread_rows(value):
        return jnp.concatenate([value] * (tall // 8), axis=0)

    def fold(value):
        out = value[:8]
        for n in range(8, value.shape[0], 8):
            out = jnp.maximum(out, value[n : n + 8])
        return out

    peaks = jnp.full((8, LANES), -jnp.inf, jnp.float32)
    for seg in range(main_segs):
        blocks = []
        for first in range(0, LANES, tall):
            at = seg * 2 * LANES + LANES + first
            ends = edges[pl.ds(at, tall), :]
            best = None
            for j in range(count):
                score = (ends - edges[pl.ds(at - widths[j], tall), :]) * spread_rows(scale[pl.ds(j * 8, 8), :])
                best = score if j == 0 else jnp.maximum(best, score)
            best = best * spread_rows(inverse)
            peaks = jnp.maximum(peaks, fold(best))
            blocks.append(best)
        turned = jnp.concatenate(blocks, axis=0).T
        for part in range(n_time):
            over[pl.ds((part * main_segs + seg) * 8, 8), :] = fold(turned[part * trials : (part + 1) * trials])
    best_all = over[pl.ds(0, total_segs, stride=8), :]
    for n in range(1, 8):
        best_all = jnp.maximum(best_all, over[pl.ds(n, total_segs, stride=8), :])
    buf[pl.ds(0, total_segs), :] = best_all
    peak_row = jnp.max(peaks, axis=0, keepdims=True)
    step = trials
    while step < LANES:
        peak_row = jnp.maximum(peak_row, pltpu.roll(peak_row, step, axis=1))
        step *= 2
    offset = first_trial % LANES
    lane = lax.broadcasted_iota(jnp.int32, (1, LANES), 1)
    peak_row = jnp.where((lane >= offset) & (lane < offset + trials), peak_row, -jnp.inf)
    for by in range(n_time):
        at = pl.multiple_of((tm ^ by) * main_segs, 8)
        outs[by][pl.ds(0, main_segs), :] = buf[pl.ds(at, main_segs), :]
        outs[by][pl.ds(main_segs, place_rows), :] = jnp.full((place_rows, LANES), -jnp.inf, jnp.float32)
        outs[by][pl.ds(main_segs + first_trial // LANES, 1), :] = peak_row


def finish_kernel(*refs, main_segs, channels):
    inputs, (best_out, peaks_out), (best, row, peaks, sems) = refs[:-6], refs[-6:-4], refs[-4:]
    merged = inputs[0][...]
    for ref in inputs[1:]:
        merged = jnp.maximum(merged, ref[...])
    best[...] = merged[:main_segs]
    row[...] = merged[main_segs:]
    first = pltpu.make_async_copy(best, best_out, sems.at[0])
    first.start()
    start = lax.axis_index("freq") * channels
    mine = pltpu.roll(row[pl.ds(start // LANES, 1), :], (LANES - start % LANES) % LANES, axis=1)
    peaks[...] = mine[:, :channels]
    second = pltpu.make_async_copy(peaks, peaks_out, sems.at[1])
    second.start()
    first.wait()
    second.wait()


def call(kernel, name, inputs, outs, scratch=(), tables=(), table_specs=SMEM, out_specs=VMEM):
    outs = [jax.ShapeDtypeStruct(out, jnp.float32) if isinstance(out, tuple) else out for out in outs]
    used = sum(4 * v.size for v in inputs) + sum(4 * math.prod(o.shape) for o in outs)
    used += sum(4 * math.prod(s.shape) for s in scratch)
    return pl.pallas_call(
        kernel,
        out_shape=outs,
        in_specs=[table_specs] * len(tables) + [VMEM] * len(inputs),
        out_specs=[out_specs] * len(outs),
        scratch_shapes=list(scratch),
        compiler_params=pltpu.CompilerParams(vmem_limit_bytes=used + (2 << 20)),
        name=name,
    )(*tables, *inputs)


def floats(rows):
    return pltpu.VMEM((rows, LANES), jnp.float32)


def shards(spectra, lead_delay, tail_delay, widths):
    channels, span = spectra.shape
    n_freq = lax.axis_size("freq")
    n_time = lax.axis_size("tm")
    freq = lax.axis_index("freq")
    sections = lead_delay.shape[0]
    local = channels.bit_length() - 1
    stages = (n_freq.bit_length() - 1) // 2
    main_segs = span // LANES
    full_time = sections - 2

    def segs_after(stage):
        spill = sum(2**s - 1 for s in range(1, local + 2 * stage + 2))
        return main_segs + -(-spill // LANES)

    def ahead_of(stage):
        return 1 + ((2 ** (local + 2 * stage + 1) - 1) >> 7)

    pairs = channels // 2
    (current,) = call(
        pair_kernel,
        "pairs",
        [spectra],
        [(pairs * main_segs, LANES)],
        [floats(channels * main_segs)],
    )
    trials = 4 * ROWS // n_time
    total_segs = n_time * main_segs
    stride = PAD + total_segs
    strides = {}
    for section in range(1, sections):
        stage = max(0, section - local) // 2
        if section >= full_time:
            strides[section] = (stride, PAD)
        else:
            strides[section] = (ahead_of(stage) + segs_after(stage), ahead_of(stage))
    windows = 1 + 3 * (stages - 1)
    shapes = [(3 * (local + 1), LANES)] + [(9, LANES)] * (stages - 1)
    *tables, widths = call(
        functools.partial(
            tables_kernel, stages=stages, sections=sections, local=local, strides=strides, trials=trials
        ),
        "tables",
        [current],
        [pltpu.SMEM(shape, jnp.int32) for shape in [*shapes, widths.shape]],
        [
            *[pltpu.VMEM(shape, jnp.int32) for shape in shapes],
            *[pltpu.VMEM((windows, sections, LANES), jnp.int32)] * 2,
            pltpu.SemaphoreType.DMA((2 * windows + 1,)),
        ],
        (lead_delay, tail_delay, widths),
        table_specs=ANY,
        out_specs=SMEM,
    )
    for stage in range(stages - 1):
        section = local + 2 * stage
        one, two, three = (xor_permute(current, "freq", by << (2 * stage)) for by in (1, 2, 3))
        ahead, segs = ahead_of(stage), segs_after(stage)
        buffers = [floats(4 * ROWS * (ahead + segs))] * 2
        inputs = [current, one, two, three]
        if stage == 0:
            (early,) = call(
                functools.partial(early_kernel, local=local, ahead=ahead, segs=segs),
                "early",
                [current, two, three],
                [(3 * ROWS * segs, LANES)],
                buffers,
                [tables[0]],
            )
            inputs = [early, one]
        (current,) = call(
            functools.partial(
                quad_kernel,
                stage=stage,
                section=section,
                local=local if stage == 0 else 0,
                ahead=ahead,
                segs=segs,
            ),
            "quad",
            inputs,
            [(ROWS * segs, LANES)],
            buffers,
            [tables[stage]],
        )
    stage = stages - 1
    two = xor_permute(current, "freq", 2 << (2 * stage))
    one = xor_permute(current, "freq", 1 << (2 * stage))
    three = xor_permute(two, "freq", 1 << (2 * stage))
    bands = [current, one, two, three]
    stacked = jnp.concatenate(bands, axis=0)
    arrays = bands + [xor_permute(stacked, "tm", by) for by in range(1, n_time)]
    peak_rows = channels * n_freq // LANES
    place_rows = -(-peak_rows // 8) * 8
    pieces = call(
        functools.partial(
            final_kernel,
            stage=stage,
            section=full_time,
            n_time=n_time,
            main_segs=main_segs,
            trials=trials,
            place_rows=place_rows,
        ),
        "final",
        arrays,
        [(main_segs + place_rows, LANES)] * n_time,
        [
            floats(4 * ROWS * stride),
            floats(2 * ROWS * stride),
            floats(trials * total_segs),
            floats(2 * LANES * main_segs),
            floats(8 * total_segs),
            floats(widths.shape[0] * 8),
        ],
        [tables[stage], widths],
    )
    merged = pieces[0]
    for by in range(1, n_time):
        merged = jnp.maximum(merged, xor_permute(pieces[by], "tm", by))
    for stage in range(stages - 1):
        received = [merged] + [xor_permute(merged, "freq", by << (2 * stage)) for by in (1, 2, 3)]
        if stage < stages - 2:
            merged = functools.reduce(jnp.maximum, received)
    best_snr, trial_peak = call(
        functools.partial(finish_kernel, main_segs=main_segs, channels=channels),
        "finish",
        received,
        [(main_segs, LANES), (1, channels)],
        [
            floats(main_segs),
            floats(place_rows),
            pltpu.VMEM((1, channels), jnp.float32),
            pltpu.SemaphoreType.DMA((2,)),
        ],
        out_specs=ANY,
    )
    return (best_snr.reshape(span), trial_peak.reshape(channels))


def solution(mesh):
    placed = (P("freq", "tm"), P(), P(), P())
    return jax.shard_map(
        shards, mesh=mesh, in_specs=placed, out_specs=(P("tm"), P("freq")), check_vma=False
    )
```

```python
import functools
import math

import jax
import jax.numpy as jnp
from jax import lax
from jax.experimental import pallas as pl
from jax.experimental.pallas import tpu as pltpu
from jax.sharding import PartitionSpec as P

LANES = 128
ROWS = 32
PAD = 8

eps_var = 1e-06
VMEM = pl.BlockSpec(memory_space=pltpu.VMEM)
ANY = pl.BlockSpec(memory_space=pl.ANY)
SMEM = pl.BlockSpec(memory_space=pltpu.SMEM)


def xor_permute(value, axis, by):
    return lax.ppermute(value, axis, [(i, i ^ by) for i in range(lax.axis_size(axis))])


def section_rows(src, dst, dst_row, segs, rows, table, entry, group=16):
    lane = lax.broadcasted_iota(jnp.int32, (segs, LANES), 1)
    for first in range(0, rows, group):
        picked = []
        for k in range(first, min(first + group, rows)):
            at, column = entry(k)
            start, delay = table[at + 1, column], table[at + 2, column]
            lower = src[pl.ds(table[at, column], segs), :]
            picked.append((k, delay, lower, src[pl.ds(start, segs), :], src[pl.ds(start - 1, segs), :]))
        for k, delay, lower, here, before in picked:
            mixed = jnp.where(lane < LANES - delay, here, before)
            dst[pl.ds(dst_row(k), segs), :] = lower + pltpu.roll(mixed, delay, axis=1)


def window(start):
    return pl.multiple_of((start // LANES) * LANES, LANES)


def order_of(freq, stage):
    order = 0
    for n in range(stage):
        order = 4 * order + ((freq >> (2 * n)) & 3)
    return order


def pair_kernel(x, out, stage):
    channels, span = x.shape
    segs = span // LANES
    half = channels // 2
    for seg in range(segs):
        stage[pl.ds(seg * channels, channels), :] = x[:, pl.ds(seg * LANES, LANES)]
    for seg in range(segs):
        first = seg * channels
        summed = stage[pl.ds(first, half, stride=2), :] + stage[pl.ds(first + 1, half, stride=2), :]
        out[pl.ds(seg, half, stride=segs), :] = summed


def stage_places(stage, section, freq, trials_first=None):
    order = order_of(freq, stage)
    place = (freq >> (2 * stage)) & 3
    rows_in = 2**section
    base = (freq >> (2 * stage + 2)) * (4 * rows_in)
    last = base + ROWS * (4 * order + place) if trials_first is None else trials_first
    half_order = (last - base) // (2 * ROWS)
    starts = [base + ROWS * half_order, base + 2 * rows_in + ROWS * half_order, last]
    return base, order, half_order, starts


def tables_kernel(widths_all, lead_all, tail_all, order_after, *refs, stages, sections, local, strides, trials):
    del order_after
    finals, widths = refs[:stages], refs[stages]
    outs, sems = refs[stages + 1 : 2 * stages + 1], refs[-1]
    freq = lax.axis_index("freq")
    plans = []
    for stage in range(stages):
        section = local + 2 * stage
        first_trial = None
        if stage == stages - 1:
            first_trial = 4 * ROWS * order_of(freq, stage) + trials * lax.axis_index("tm")
        base, order, half_order, starts = stage_places(stage, section, freq, first_trial)
        plans.append((section, order, half_order, [base] if stage == 0 else starts))
    places = [window(where) for *_, wheres in plans for where in wheres]
    lane = lax.broadcasted_iota(jnp.int32, (1, LANES), 1)

    def by_distance(value):
        for bit, width in enumerate((ROWS, 2 * ROWS)):
            ahead = pltpu.roll(value, LANES - width, axis=1)
            swapped = jnp.where((lane // width) % 2 == 0, ahead, pltpu.roll(value, width, axis=1))
            value = jnp.where(((freq >> bit) & 1) == 1, swapped, value)
        return value

    slot = 0
    for stage, (section, order, half_order, wheres) in enumerate(plans):
        out, at = outs[stage], 0
        jobs = []
        if stage == 0:
            for now in range(1, local):
                band = lane // (2 * 2**now)
                rows = (2 * band, 2 * band + 1) if now == 1 else (2 * band * 2**now, (2 * band + 1) * 2**now)
                jobs.append((slot, now, *rows, now > 1, strides[now]))
            band = lane // (2 * ROWS)
            place = freq & 3
            rows = ((2 * band) ^ place) * ROWS, ((2 * band + 1) ^ place) * ROWS
            jobs.append((slot, section, *rows, True, strides[section]))
            jobs.append((slot, section + 1, -ROWS * half_order, ROWS - ROWS * half_order, True, strides[section + 1]))
        else:
            for band in range(2):
                low = 2 * band * ROWS - ROWS * order
                jobs.append((slot + band, section, low, low + ROWS, True, strides[section]))
            low = -ROWS * half_order
            jobs.append((slot + 2, section + 1, low, low + ROWS, True, strides[section + 1]))
        for where, row, low, up, picks, (stride, ahead) in jobs:
            part = (pl.ds(row, 1), pl.ds(places[where], LANES))
            e, h = lead_all[part], tail_all[part]
            if row < section:
                e, h = by_distance(e), by_distance(h)
            out[pl.ds(at, 1), :] = (low + e if picks else low) * stride + ahead
            out[pl.ds(at + 1, 1), :] = (up + h if picks else up) * stride + ahead - (e >> 7)
            out[pl.ds(at + 2, 1), :] = e & (LANES - 1)
            at += 3
        slot += len(wheres)
    copies = [pltpu.make_async_copy(outs[n], finals[n], sems.at[n]) for n in range(stages)]
    copies.append(pltpu.make_async_copy(widths_all, widths, sems.at[stages]))
    for copy in copies:
        copy.start()
    for copy in copies:
        copy.wait()


def local_sections(table, pieces, buf_a, buf_b, local, ahead, segs, out=None):
    stride = ahead + segs
    half = ROWS // 2
    for buf in (buf_a, buf_b):
        buf[...] = jnp.zeros(buf.shape, jnp.float32)
    for by, ref in pieces:
        in_segs = ref.shape[0] // half
        to = by * (half * stride) + ahead
        for row in range(half):
            buf_a[pl.ds(to + row * stride, in_segs), :] = ref[pl.ds(row * in_segs, in_segs), :]
    src, dst = buf_a, buf_b
    for now in range(1, local):
        to_out = out is not None and now == local - 1
        for n, (by, _) in enumerate(pieces):
            base = by * ROWS
            first, step = (n * ROWS * segs, segs) if to_out else (base * stride + ahead, stride)
            section_rows(
                src,
                out if to_out else dst,
                lambda k, first=first, step=step: first + k * step,
                segs,
                ROWS,
                table,
                lambda k, now=now, base=base: (3 * (now - 1), base + k),
            )
        src, dst = dst, src
    return src, dst


def early_kernel(table, own, two, three, out, buf_a, buf_b, *, local, ahead, segs):
    local_sections(table, [(0, own), (2, two), (3, three)], buf_a, buf_b, local, ahead, segs, out)


def quad_kernel(table, *refs, stage, section, local, ahead, segs):
    *inputs, out, buf_a, buf_b = refs
    freq = lax.axis_index("freq")
    place = (freq >> (2 * stage)) & 3
    _, _, half_order, starts = stage_places(stage, section, freq)
    stride = ahead + segs

    def at_row(k):
        return k * stride + ahead

    if local:
        early, late = inputs
        src, dst = local_sections(table, [(1, late)], buf_a, buf_b, local, ahead, segs)
        ready = [(by, early, n * ROWS * segs, segs) for n, by in enumerate((0, 2, 3))]
    else:
        src, dst = buf_a, buf_b
        for buf in (buf_a, buf_b):
            buf[...] = jnp.zeros(buf.shape, jnp.float32)
        ready = [(by, ref, 0, ref.shape[0] // ROWS) for by, ref in enumerate(inputs)]
    for by, ref, at, in_segs in ready:
        to = (by if local else place ^ by) * (ROWS * stride) + ahead
        for row in range(ROWS):
            src[pl.ds(to + row * stride, in_segs), :] = ref[pl.ds(at + row * in_segs, in_segs), :]

    def mid_entry(k):
        band = k // ROWS
        if local:
            return 3 * (local - 1), 2 * ROWS * band + ROWS * half_order + k % ROWS
        return 3 * band, starts[band] % LANES + k % ROWS

    section_rows(src, dst, at_row, segs, 2 * ROWS, table, mid_entry)
    at = 3 * local if local else 6
    column = starts[2] % LANES
    section_rows(dst, out, lambda k: k * segs, segs, ROWS, table, lambda k: (at, column + k))


def final_kernel(table, widths, *refs, stage, section, n_time, main_segs, trials, place_rows):
    own, moved = refs[:4], refs[4 : 3 + n_time]
    outs = refs[3 + n_time : 3 + 2 * n_time]
    buf, mid, data, edges, over, scale = refs[3 + 2 * n_time :]
    freq = lax.axis_index("freq")
    tm = lax.axis_index("tm")
    place = (freq >> (2 * stage)) & 3
    first_trial = 4 * ROWS * order_of(freq, stage) + trials * tm
    _, _, _, starts = stage_places(stage, section, freq, first_trial)
    total_segs = n_time * main_segs
    total_time = total_segs * LANES
    stride = PAD + total_segs
    zeros = jnp.zeros((PAD, LANES), jnp.float32)
    for row in range(4 * ROWS):
        buf[pl.ds(row * stride, PAD), :] = zeros
    for row in range(2 * ROWS):
        mid[pl.ds(row * stride, PAD), :] = zeros
    in_segs = own[0].shape[0] // ROWS
    size = ROWS * in_segs
    sources = []
    for by_band in range(4):
        for by_time in range(n_time):
            start = (place ^ by_band) * (ROWS * stride) + PAD
            part = tm ^ by_time
            ref, at = (own[by_band], 0) if by_time == 0 else (moved[by_time - 1], by_band * size)
            sources.append((start, part, ref, at))
    for start, part, ref, at in sources:
        for row in range(ROWS):
            to = pl.multiple_of(start + part * main_segs + row * stride, 8)
            buf[pl.ds(to, main_segs), :] = ref[pl.ds(at + row * in_segs, main_segs), :]
    for start, part, ref, at in sources:
        to = start + jnp.minimum(part + 1, n_time - 1) * main_segs
        for seg in range(in_segs - main_segs):
            spill = ref[pl.ds(at + main_segs + seg, ROWS, stride=in_segs), :]
            where = pl.ds(to + seg, ROWS, stride=stride)
            buf[where, :] = buf[where, :] + jnp.where(part + 1 < n_time, spill, 0.0)

    section_rows(
        buf,
        mid,
        lambda k: PAD + k * stride,
        total_segs,
        2 * ROWS,
        table,
        lambda k: (3 * (k // ROWS), starts[k // ROWS] % LANES + k % ROWS),
    )
    column = first_trial % LANES
    section_rows(mid, data, lambda k: k * total_segs, total_segs, trials, table, lambda k: (6, column + k))

    def samples(seg):
        return data[pl.ds(seg, trials, stride=total_segs), :]

    total = samples(0)
    for seg in range(1, total_segs):
        total = total + samples(seg)
    mean = jnp.sum(total, axis=1, keepdims=True) / total_time

    row_at = lax.broadcasted_iota(jnp.int32, (2 * LANES, LANES), 0)
    column_at = lax.broadcasted_iota(jnp.int32, (2 * LANES, LANES), 1)
    after = jnp.where(column_at > row_at, -1.0, 0.0)
    upto = jnp.where(column_at <= row_at - LANES, 1.0, 0.0)
    ones = jnp.where(row_at < LANES, after, upto).astype(jnp.bfloat16)
    ones = jnp.concatenate([ones] * 3, axis=1)
    squares = jnp.zeros((trials, LANES), jnp.float32)
    for seg in range(-1, main_segs):
        parts = []
        for part in range(n_time):
            at = part * main_segs + seg
            centred = samples(at) - mean if at >= 0 else jnp.zeros((trials, LANES), jnp.float32)
            if seg >= 0:
                squares = squares + centred * centred
            parts.append(centred)
        values = jnp.concatenate(parts, axis=0)
        terms = []
        for _ in range(3):
            term = values.astype(jnp.bfloat16)
            terms.append(term)
            values = values - term.astype(jnp.float32)
        both = lax.dot_general(
            ones,
            jnp.concatenate(terms, axis=1),
            (((1,), (1,)), ((), ())),
            preferred_element_type=jnp.float32,
        )
        if seg + 1 < main_segs:
            edges[pl.ds((seg + 1) * 2 * LANES, LANES), :] = both[:LANES]
        if seg >= 0:
            edges[pl.ds(seg * 2 * LANES + LANES, LANES), :] = both[LANES:]
    squares = jnp.sum(squares, axis=1, keepdims=True)
    inverse = 1.0 / jnp.sqrt(squares / total_time + eps_var)
    inverse = jnp.concatenate([jnp.broadcast_to(inverse, (trials, LANES))] * n_time, axis=0).T[:8]

    count = widths.shape[0]
    for j in range(count):
        scale[pl.ds(j * 8, 8), :] = jnp.full((8, LANES), widths[j], jnp.int32).astype(jnp.float32)
    scale[...] = 1.0 / jnp.sqrt(scale[...])
    tall = 64

    def spread_rows(value):
        return jnp.concatenate([value] * (tall // 8), axis=0)

    def fold(value):
        out = value[:8]
        for n in range(8, value.shape[0], 8):
            out = jnp.maximum(out, value[n : n + 8])
        return out

    peaks = jnp.full((8, LANES), -jnp.inf, jnp.float32)
    for seg in range(main_segs):
        blocks = []
        for first in range(0, LANES, tall):
            at = seg * 2 * LANES + LANES + first
            ends = edges[pl.ds(at, tall), :]
            best = None
            for j in range(count):
                score = (ends - edges[pl.ds(at - widths[j], tall), :]) * spread_rows(scale[pl.ds(j * 8, 8), :])
                best = score if j == 0 else jnp.maximum(best, score)
            best = best * spread_rows(inverse)
            peaks = jnp.maximum(peaks, fold(best))
            blocks.append(best)
        turned = jnp.concatenate(blocks, axis=0).T
        for part in range(n_time):
            over[pl.ds((part * main_segs + seg) * 8, 8), :] = fold(turned[part * trials : (part + 1) * trials])
    best_all = over[pl.ds(0, total_segs, stride=8), :]
    for n in range(1, 8):
        best_all = jnp.maximum(best_all, over[pl.ds(n, total_segs, stride=8), :])
    buf[pl.ds(0, total_segs), :] = best_all
    peak_row = jnp.max(peaks, axis=0, keepdims=True)
    step = trials
    while step < LANES:
        peak_row = jnp.maximum(peak_row, pltpu.roll(peak_row, step, axis=1))
        step *= 2
    offset = first_trial % LANES
    lane = lax.broadcasted_iota(jnp.int32, (1, LANES), 1)
    peak_row = jnp.where((lane >= offset) & (lane < offset + trials), peak_row, -jnp.inf)
    for by in range(n_time):
        at = pl.multiple_of((tm ^ by) * main_segs, 8)
        outs[by][pl.ds(0, main_segs), :] = buf[pl.ds(at, main_segs), :]
        outs[by][pl.ds(main_segs, place_rows), :] = jnp.full((place_rows, LANES), -jnp.inf, jnp.float32)
        outs[by][pl.ds(main_segs + first_trial // LANES, 1), :] = peak_row


def finish_kernel(*refs, main_segs, channels):
    inputs, (best_out, peaks_out), (best, row, peaks, sems) = refs[:-6], refs[-6:-4], refs[-4:]
    merged = inputs[0][...]
    for ref in inputs[1:]:
        merged = jnp.maximum(merged, ref[...])
    best[...] = merged[:main_segs]
    row[...] = merged[main_segs:]
    first = pltpu.make_async_copy(best, best_out, sems.at[0])
    first.start()
    start = lax.axis_index("freq") * channels
    mine = pltpu.roll(row[pl.ds(start // LANES, 1), :], (LANES - start % LANES) % LANES, axis=1)
    peaks[...] = mine[:, :channels]
    second = pltpu.make_async_copy(peaks, peaks_out, sems.at[1])
    second.start()
    first.wait()
    second.wait()


def call(kernel, name, inputs, outs, scratch=(), tables=(), table_specs=SMEM, out_specs=VMEM):
    outs = [jax.ShapeDtypeStruct(out, jnp.float32) if isinstance(out, tuple) else out for out in outs]
    used = sum(4 * v.size for v in inputs) + sum(4 * math.prod(o.shape) for o in outs)
    used += sum(4 * math.prod(s.shape) for s in scratch)
    return pl.pallas_call(
        kernel,
        out_shape=outs,
        in_specs=[table_specs] * len(tables) + [VMEM] * len(inputs),
        out_specs=[out_specs] * len(outs),
        scratch_shapes=list(scratch),
        compiler_params=pltpu.CompilerParams(vmem_limit_bytes=used + (2 << 20)),
        name=name,
    )(*tables, *inputs)


def floats(rows):
    return pltpu.VMEM((rows, LANES), jnp.float32)


def shards(spectra, lead_delay, tail_delay, widths):
    channels, span = spectra.shape
    n_freq = lax.axis_size("freq")
    n_time = lax.axis_size("tm")
    freq = lax.axis_index("freq")
    sections = lead_delay.shape[0]
    local = channels.bit_length() - 1
    stages = (n_freq.bit_length() - 1) // 2
    main_segs = span // LANES
    full_time = sections - 2

    def segs_after(stage):
        spill = sum(2**s - 1 for s in range(1, local + 2 * stage + 2))
        return main_segs + -(-spill // LANES)

    def ahead_of(stage):
        return 1 + ((2 ** (local + 2 * stage + 1) - 1) >> 7)

    pairs = channels // 2
    (current,) = call(
        pair_kernel,
        "pairs",
        [spectra],
        [(pairs * main_segs, LANES)],
        [floats(channels * main_segs)],
    )
    trials = 4 * ROWS // n_time
    total_segs = n_time * main_segs
    stride = PAD + total_segs
    strides = {}
    for section in range(1, sections):
        stage = max(0, section - local) // 2
        if section >= full_time:
            strides[section] = (stride, PAD)
        else:
            strides[section] = (ahead_of(stage) + segs_after(stage), ahead_of(stage))
    shapes = [(3 * (local + 1), LANES)] + [(9, LANES)] * (stages - 1)
    *tables, widths = call(
        functools.partial(
            tables_kernel, stages=stages, sections=sections, local=local, strides=strides, trials=trials
        ),
        "tables",
        [lead_delay, tail_delay, current],
        [pltpu.SMEM(shape, jnp.int32) for shape in [*shapes, widths.shape]],
        [
            *[pltpu.VMEM(shape, jnp.int32) for shape in shapes],
            pltpu.SemaphoreType.DMA((stages + 1,)),
        ],
        [widths],
        table_specs=ANY,
        out_specs=SMEM,
    )
    for stage in range(stages - 1):
        section = local + 2 * stage
        one, two, three = (xor_permute(current, "freq", by << (2 * stage)) for by in (1, 2, 3))
        ahead, segs = ahead_of(stage), segs_after(stage)
        buffers = [floats(4 * ROWS * (ahead + segs))] * 2
        inputs = [current, one, two, three]
        if stage == 0:
            (early,) = call(
                functools.partial(early_kernel, local=local, ahead=ahead, segs=segs),
                "early",
                [current, two, three],
                [(3 * ROWS * segs, LANES)],
                buffers,
                [tables[0]],
            )
            inputs = [early, one]
        (current,) = call(
            functools.partial(
                quad_kernel,
                stage=stage,
                section=section,
                local=local if stage == 0 else 0,
                ahead=ahead,
                segs=segs,
            ),
            "quad",
            inputs,
            [(ROWS * segs, LANES)],
            buffers,
            [tables[stage]],
        )
    stage = stages - 1
    two = xor_permute(current, "freq", 2 << (2 * stage))
    one = xor_permute(current, "freq", 1 << (2 * stage))
    three = xor_permute(two, "freq", 1 << (2 * stage))
    bands = [current, one, two, three]
    stacked = jnp.concatenate(bands, axis=0)
    arrays = bands + [xor_permute(stacked, "tm", by) for by in range(1, n_time)]
    peak_rows = channels * n_freq // LANES
    place_rows = -(-peak_rows // 8) * 8
    pieces = call(
        functools.partial(
            final_kernel,
            stage=stage,
            section=full_time,
            n_time=n_time,
            main_segs=main_segs,
            trials=trials,
            place_rows=place_rows,
        ),
        "final",
        arrays,
        [(main_segs + place_rows, LANES)] * n_time,
        [
            floats(4 * ROWS * stride),
            floats(2 * ROWS * stride),
            floats(trials * total_segs),
            floats(2 * LANES * main_segs),
            floats(8 * total_segs),
            floats(widths.shape[0] * 8),
        ],
        [tables[stage], widths],
    )
    merged = pieces[0]
    for by in range(1, n_time):
        merged = jnp.maximum(merged, xor_permute(pieces[by], "tm", by))
    for stage in range(stages - 1):
        received = [merged] + [xor_permute(merged, "freq", by << (2 * stage)) for by in (1, 2, 3)]
        if stage < stages - 2:
            merged = functools.reduce(jnp.maximum, received)
    best_snr, trial_peak = call(
        functools.partial(finish_kernel, main_segs=main_segs, channels=channels),
        "finish",
        received,
        [(main_segs, LANES), (1, channels)],
        [
            floats(main_segs),
            floats(place_rows),
            pltpu.VMEM((1, channels), jnp.float32),
            pltpu.SemaphoreType.DMA((2,)),
        ],
        out_specs=ANY,
    )
    return (best_snr.reshape(span), trial_peak.reshape(channels))


def solution(mesh):
    placed = (P("freq", "tm"), P(), P(), P())
    return jax.shard_map(
        shards, mesh=mesh, in_specs=placed, out_specs=(P("tm"), P("freq")), check_vma=False
    )
```
